32 devices in a mesh: sub: 8 (over z, y), sec: 4 (over x, core).
Axes of the slice: x: 2, y: 2, z: 4, core: 2. Of those that a mesh axis runs over, the one named last changes fastest.
Arguments:
- start_vectors: bfloat16 [32, 3, 256, 512], P(None, None, 'sub', 'sec'), may hold values from -6 to 6
- stiffness: bfloat16 [3, 256, 512], P(None, 'sub', 'sec'), may hold values from 1.5 to 15
- coupling: bfloat16 [256, 512], P('sub', 'sec'), may hold values from -0.5 to 0.5
- kept_ranks: int32 [8, 4], P('sub', 'sec'), may hold values from 16 to 32, as said below
- level_start: float32 [256, 16], P('sub'), may hold values from -6 to 6
Outputs:
- prolonged: float32 [16, 3, 256, 512], P(None, None, 'sub', 'sec')
The draws below stay inside these ranges and needn't reach their ends.
Inputs may be any that keep to these rules, and one draw needn't show every extreme that they name: `kept_ranks`: every subdomain keeps at least half of its 32 vectors; some subdomain keeps all 32 and some keeps exactly half.
All inputs are finite; a program needn't handle non-finite values.
Results may differ from the reference program's by a relative error of at most 0.0003.
Values may be sent and summed in bfloat16 or wider, within the bound.
No kernel may reach another device: no remote copies, remote signals or barrier semaphores. Data moves between devices by JAX's collectives and lax.ppermute only.
A program may use at most 64 MiB of HBM per device.

```python
import math
import jax
import jax.numpy as jnp
from jax import lax

CX = 32
H = 4
CY = 128
NV = 32
K2 = 16
ITERS = 2
LEVEL_ITERS = 2
SPANS = 8
SECTS = 4
NX = 256
NY = 512
XEXT = 40
YEXT = 136


def draw_kept_ranks(key, part):
    total = SPANS * SECTS
    values = jax.random.randint(jax.random.fold_in(key, 11), (total,), NV // 2, NV + 1)
    where = jax.random.randint(jax.random.fold_in(key, 12), (), 0, total)
    values = values.at[where].set(NV)
    values = values.at[(where + 1) % total].set(NV // 2)
    return values.reshape(SPANS, SECTS).astype(jnp.int32)


def levels(own_key, shape, shards, least, high):
    loudness = 1.0
    for dim, blocks in shards:
        steps = jax.random.uniform(jax.random.fold_in(jax.random.fold_in(own_key, 6), dim), (blocks,), jnp.float32, least / len(shards), high / len(shards))
        loudness = loudness * jnp.repeat(jnp.exp(steps), shape[dim] // blocks).reshape((-1,) + (1,) * (len(shape) - 1 - dim))
    return loudness


def scatter_about(own_key, shape, deviation, most, split=(), held_as=jnp.bfloat16):
    loudness = levels(own_key, shape, split, -0.22, 0.18) if split else 1.0
    array = jax.random.normal(own_key, shape, jnp.float32) * deviation * loudness
    return jnp.minimum(jnp.maximum(array, -most), most).astype(held_as)


def setup_inputs(seed: int = 0) -> dict:
    seeds = jax.random.split(jax.random.key(seed), 6)
    return {
        "start_vectors": scatter_about(seeds[0], (NV, 3, NX, NY), 1.0, 6.0, ((2, 8), (3, 4))),
        "stiffness": jnp.clip(jnp.exp(math.log(15.0) - 2.3025851 * jax.random.uniform(seeds[1], (3, NX, NY), jnp.float32) ** levels(seeds[1], (3, NX, NY), ((1, 8), (2, 4)), -0.2, 0.2)), 1.5, 15.0).astype(jnp.bfloat16),
        "coupling": jnp.clip(jax.random.uniform(seeds[2], (NX, NY), jnp.float32, -0.5, 0.5) * levels(seeds[2], (NX, NY), ((0, 8), (1, 4)), -0.4, 0.0), -0.5, 0.5).astype(jnp.bfloat16),
        "kept_ranks": draw_kept_ranks(jax.random.fold_in(seeds[5], 71), 0),
        "level_start": scatter_about(seeds[4], (SPANS * NV, K2), 1.0, 6.0, ((0, 8),), jnp.float32),
    }


highest = lax.Precision.HIGHEST

def apply_operator(vectors, stiff_diag, shear_term, inside):
    padded = jnp.pad(vectors, ((0, 0), (0, 0), (1, 1), (1, 1)))
    beside = padded[:, :, 2:, 1:-1] + padded[:, :, :-2, 1:-1] + padded[:, :, 1:-1, 2:] + padded[:, :, 1:-1, :-2]
    others = lax.optimization_barrier(jnp.sum(vectors, axis=1, keepdims=True)) - vectors
    return ((4.0 + stiff_diag) * vectors - beside + shear_term * others) * inside

def orthonormal(work):
    shape_before = work.shape
    flat = work.reshape(shape_before[0], -1)
    gram = jnp.dot(flat, flat.T, precision=highest)
    lower = jnp.linalg.cholesky(gram)
    solved = lax.linalg.triangular_solve(lower, flat, left_side=True, lower=True)
    return solved.reshape(shape_before)

def subspace_basis(vectors, stiff_diag, shear_term, inside, rank):
    for iteration in range(ITERS):
        vectors = orthonormal(apply_operator(vectors, stiff_diag, shear_term, inside))
    live = (jnp.arange(NV, dtype=jnp.int32) < rank).astype(jnp.float32)
    basis = vectors * live[:, None, None, None]
    image = apply_operator(basis, stiff_diag, shear_term, inside)
    self_block = jnp.dot(basis.reshape(NV, -1), image.reshape(NV, -1).T, precision=highest)
    return (basis, self_block)

def level_basis(self_blocks, couple_blocks, level_start):
    rows = level_start.reshape(-1, NV, K2)
    span_count = rows.shape[0]
    zero_block = jnp.zeros((1, NV, NV), jnp.float32)
    couple_prev = jnp.concatenate([zero_block, couple_blocks[:-1]], axis=0)
    zero_rows = jnp.zeros((1, NV, K2), jnp.float32)
    for iteration in range(LEVEL_ITERS):
        rows_next = jnp.concatenate([rows[1:], zero_rows], axis=0)
        rows_prev = jnp.concatenate([zero_rows, rows[:-1]], axis=0)
        image = jnp.einsum('sab,sbk->sak', self_blocks, rows, precision=highest)
        image = image + jnp.einsum('sab,sbk->sak', couple_blocks, rows_next, precision=highest)
        image = image + jnp.einsum('sba,sbk->sak', couple_prev, rows_prev, precision=highest)
        flat = image.reshape(span_count * NV, K2)
        gram = jnp.dot(flat.T, flat, precision=highest)
        lower = jnp.linalg.cholesky(gram)
        solved = lax.linalg.triangular_solve(lower, flat.T, left_side=True, lower=True)
        rows = solved.T.reshape(span_count, NV, K2)
    return rows

def reference(start_vectors, stiffness, coupling, kept_ranks, level_start):
    margins = ((H, H), (H, H))
    start_pad = jnp.pad(start_vectors.astype(jnp.float32), ((0, 0), (0, 0)) + margins)
    stiff_pad = jnp.pad(stiffness.astype(jnp.float32), ((0, 0),) + margins)
    shear_pad = jnp.pad(coupling.astype(jnp.float32), margins)
    inside_pad = jnp.pad(jnp.ones((NX, NY), jnp.float32), margins)
    anchor = jnp.zeros((), jnp.int32)

    def one_domain(flat_index):
        span_index = flat_index // SECTS
        sect_index = flat_index % SECTS
        row_start = (span_index * CX).astype(jnp.int32)
        col_start = (sect_index * CY).astype(jnp.int32)
        vectors = lax.dynamic_slice(start_pad, (anchor, anchor, row_start, col_start), (NV, 3, XEXT, YEXT))
        stiff_diag = lax.dynamic_slice(stiff_pad, (anchor, row_start, col_start), (3, XEXT, YEXT))
        shear_term = lax.dynamic_slice(shear_pad, (row_start, col_start), (XEXT, YEXT))
        inside = lax.dynamic_slice(inside_pad, (row_start, col_start), (XEXT, YEXT))
        rank = kept_ranks[span_index, sect_index]
        basis, self_block = subspace_basis(vectors, stiff_diag, shear_term, inside, rank)
        upper_rim = (4.0 + stiff_diag[:, CX:, :]) * basis[:, :, CX:, :]
        lower_rim = basis[:, :, :2 * H, :]
        owned = basis[:, :, H:H + CX, H:H + CY]
        return (self_block, upper_rim, lower_rim, owned)
    self_blocks, upper_rims, lower_rims, owned = lax.map(one_domain, jnp.arange(SPANS * SECTS, dtype=jnp.int32))
    self_blocks = self_blocks.reshape(SPANS, SECTS, NV, NV)
    upper_rims = upper_rims.reshape(SPANS, SECTS, NV, 3, 2 * H, YEXT)
    lower_rims = lower_rims.reshape(SPANS, SECTS, NV, 3, 2 * H, YEXT)
    lower_next = jnp.concatenate([lower_rims[1:], jnp.zeros((1, SECTS, NV, 3, 2 * H, YEXT), jnp.float32)], axis=0)
    couple_blocks = jnp.einsum('stacxy,stbcxy->stab', upper_rims, lower_next, precision=highest)
    level_rows = jax.vmap(level_basis, in_axes=(1, 1, None), out_axes=1)(self_blocks, couple_blocks, level_start)
    owned = owned.reshape(SPANS, SECTS, NV, 3, CX, CY)
    factor = math.sqrt(SPANS * 3 * XEXT * YEXT)
    prolonged = factor * jnp.einsum('stak,stacxy->kcsxty', level_rows, owned, precision=highest)
    return prolonged.reshape(K2, 3, NX, NY)
```

```python
import math

import jax
import jax.numpy as jnp
from jax import lax
from jax.experimental import pallas as pl
from jax.experimental.pallas import tpu as pltpu
from jax.sharding import PartitionSpec as P

H = 4
REACH = H + 2
MIB = 1 << 20
F32 = jnp.float32
BF16 = jnp.bfloat16
NN = (((1,), (0,)), ((), ()))
NT = (((1,), (1,)), ((), ()))
TN = (((0,), (0,)), ((), ()))


def iota(shape, dim):
    return lax.broadcasted_iota(jnp.int32, shape, dim)


def split(x):
    high = x.astype(BF16)
    return high, (x - high.astype(F32)).astype(BF16)


def dot(a, b, dims):
    return lax.dot_general(a, b, dims, preferred_element_type=F32)


def dot3(a, b, dims):
    (ah, al), (bh, bl) = split(a), split(b)
    return dot(ah, bh, dims) + (dot(ah, bl, dims) + dot(al, bh, dims))


def inverse_factor(gram, size):
    row, lane = iota((size, 128), 0), iota((size, 128), 1)
    work = jnp.where(lane < size, gram, jnp.where(lane == row + size, 1.0, 0.0))
    for j in range(size - 1):
        column = work[:, j : j + 1]
        pivot = work[j : j + 1, :]
        factor = jnp.where(iota((size, 1), 0) > j, column / column[j : j + 1, :], 0.0)
        work = work - factor * pivot
    diag = jnp.sum(jnp.where(lane == row, work, 0.0), axis=1, keepdims=True)
    return pltpu.roll(work / jnp.sqrt(diag), 128 - size, 1)


def pack_kernel(v_ref, k_ref, g_ref, own_ref, sec_ref, sub_ref, vf, kf):
    nv, comps, cx, cy = v_ref.shape
    sub_even = lax.rem(lax.axis_index("sub"), 2) == 0
    sec_even = lax.rem(lax.axis_index("sec"), 2) == 0
    vf[...] = v_ref[...].astype(F32).reshape(vf.shape)
    kf[...] = jnp.zeros(kf.shape, F32)
    kf[: comps * cx] = k_ref[...].astype(F32).reshape(comps * cx, cy)
    kf[comps * cx : (comps + 1) * cx] = g_ref[...].astype(F32)
    group = iota((nv, cy), 1) // H
    for c in range(comps + 1):
        left = jnp.zeros((nv, cy), F32)
        right = jnp.zeros((nv, cy), F32)
        for x in range(cx):
            if c < comps:
                tile = vf[pl.ds(c * cx + x, nv, stride=comps * cx), :]
            else:
                tile = jnp.concatenate([kf[pl.ds(x, 8, stride=cx), :], jnp.zeros((nv - 8, cy), F32)], axis=0)
            own_ref[x, c] = tile.astype(BF16)
            rolled = pltpu.roll(tile, H * x, 1) if x else tile
            left = jnp.where(group == x, rolled, left)
            right = jnp.where(group == (x + cx - 1) % cx, rolled, right)
        sec_ref[0, c] = jnp.where(sec_even, right, left).astype(BF16)
        sec_ref[1, c] = jnp.where(sec_even, left, right).astype(BF16)
    last = cx - REACH
    sub_ref[0] = own_ref[pl.ds(jnp.where(sub_even, last, 0), REACH)]
    sub_ref[1] = own_ref[pl.ds(jnp.where(sub_even, 0, last), REACH)]


def fine_kernel(sizes, rank_ref, start_ref, own_ref, sec_a, sec_b, sub_a, sub_b, pack_ref, basis_ref, v0, x1, x2, s1, coef, acc, facc):
    spans, sects = sizes
    cx, channels, nv, cy = own_ref.shape
    comps = channels - 1
    wide = 2 * cy
    s, t = lax.axis_index("sub"), lax.axis_index("sec")
    sub_even, sec_even = lax.rem(s, 2) == 0, lax.rem(t, 2) == 0
    lane = iota((nv, cy), 1)
    group = lane // H
    first, last = lane < H, lane >= cy - H

    def tail(hi, lo, x):
        rolled = jnp.where(group == x, hi, lo)
        rolled = pltpu.roll(rolled, cy - H * x, 1) if x else rolled
        return jnp.where(first | last, rolled, 0.0)

    sublane = iota((8, wide), 0)
    wide_lane = iota((1, wide), 1)
    col_in = (wide_lane < cy) | ((wide_lane < cy + H) & (t < sects - 1)) | ((wide_lane >= wide - H) & (t > 0))

    def put(x, c, main, side):
        both = jnp.concatenate([main, side], axis=1)
        if c < comps:
            v0[x + H, c] = both
        else:
            both = both[:8]
            row_in = True if 0 <= x < cx else (s > 0 if x < 0 else s < spans - 1)
            inside = jnp.where(col_in & row_in, 1.0, 0.0)
            g = both[comps : comps + 1]
            terms = jnp.where(sublane < comps, 4.0 + both - g, jnp.where(sublane == comps, both, 1.0))
            coef[x + H] = terms * inside

    def halves(ref_a, ref_b, even, index):
        a, b = ref_a[index].astype(F32), ref_b[index].astype(F32)
        return jnp.where(even, a, b), jnp.where(even, b, a)

    for c in range(channels):
        hi, lo = halves(sec_a, sec_b, sec_even, c)
        for x in range(cx):
            put(x, c, own_ref[x, c].astype(F32), tail(hi, lo, x))
        after_hi, before_hi = halves(sub_a, sub_b, sub_even, (REACH, c))
        after_lo, before_lo = halves(sub_a, sub_b, sub_even, (REACH + 1, c))
        after_hi, after_lo = jnp.where(sec_even, after_hi, after_lo), jnp.where(sec_even, after_lo, after_hi)
        before_hi, before_lo = jnp.where(sec_even, before_hi, before_lo), jnp.where(sec_even, before_lo, before_hi)
        for i in range(REACH):
            after, before = halves(sub_a, sub_b, sub_even, (i, c))
            put(cx + i, c, after, tail(after_hi, after_lo, i))
            if i >= REACH - H:
                x = i - REACH
                put(x, c, before, tail(before_hi, before_lo, cx + x))

    def operator_row(src, i, k, emit, up=True, down=True):
        diag = [jnp.broadcast_to(coef[k, c : c + 1, :], (8, wide)) for c in range(comps)]
        shear = jnp.broadcast_to(coef[k, comps : comps + 1, :], (8, wide))
        mask = jnp.broadcast_to(coef[k, comps + 1 : comps + 2, :], (8, wide))
        for o in range(nv // 8):
            rows = slice(8 * o, 8 * o + 8)
            v = [src[i, c, rows, :] for c in range(comps)]
            total = shear * (v[0] + v[1] + v[2])
            for c in range(comps):
                beside = pltpu.roll(v[c], 1, 1) + pltpu.roll(v[c], wide - 1, 1)
                if up:
                    beside = beside + src[i - 1, c, rows, :]
                if down:
                    beside = beside + src[i + 1, c, rows, :]
                emit(c, rows, diag[c] * v[c] + total - mask * beside)

    def operator(src, dst, count, coef_row, tail_down=False):
        def body(i, carry, up=True, down=True):
            def emit(c, rows, value):
                dst[i, c, rows, :] = value
            operator_row(src, i, i + coef_row, emit, up, down)
            return carry
        body(0, 0, up=False)
        lax.fori_loop(1, count if tail_down else count - 1, body, 0)
        if not tail_down:
            body(count - 1, 0, down=False)

    rows_ext = cx + 2 * H
    operator(v0, x1, rows_ext, 0)
    operator(x1, x2, rows_ext, 0)

    acc[...] = jnp.zeros(acc.shape, F32)

    def gram_row(i, carry, up=True, down=True):
        images = {}
        def emit(c, rows, value):
            images.setdefault(c, []).append(value)
        operator_row(x2, i, i, emit, up, down)
        total = carry
        for c in range(comps):
            h2, l2 = split(x2[i, c])
            h3, l3 = split(jnp.concatenate(images[c], axis=0))
            two = jnp.concatenate([h2, l2], axis=0)
            four = jnp.concatenate([two, h3, l3], axis=0)
            total = total + dot(two, four, NT)
        return total
    total = gram_row(0, jnp.zeros((2 * nv, 4 * nv), F32), up=False)
    total = lax.fori_loop(1, rows_ext - 1, gram_row, total)
    total = gram_row(rows_ext - 1, total, down=False)
    total = total[:nv] + total[nv:]
    total = total + pltpu.roll(total, 4 * nv - nv, 1)
    gram = total

    base = cx
    operator(v0.at[pl.ds(base, 2 * H + 2)], s1, 2 * H + 1, base, tail_down=True)

    def rim_row(i, carry, up=True):
        images = {}
        def emit(c, rows, value):
            images.setdefault(c, []).append(value)
        operator_row(s1, i, i + base, emit, up, True)
        total = carry
        for c in range(comps):
            stiff = jnp.broadcast_to(coef[i + base, c : c + 1, :] + coef[i + base, comps : comps + 1, :], (nv, wide))
            a = jnp.concatenate(split(x2[i + base, c] * stiff), axis=0)
            b = jnp.concatenate(split(jnp.concatenate(images[c], axis=0)), axis=0)
            total = total + dot(a, b, NT)
        return total
    rim = rim_row(0, jnp.zeros((2 * nv, 2 * nv), F32), up=False)
    rim = lax.fori_loop(1, 2 * H, rim_row, rim)
    rim = rim[:nv] + rim[nv:]
    rim = rim[:, :nv] + rim[:, nv:]
    rim = jnp.where(s < spans - 1, rim, 0.0)

    inverse = inverse_factor(gram, nv)[:, :nv]
    inverse = jnp.where(iota((nv, nv), 0) < rank_ref[0, 0], inverse, 0.0)
    start = start_ref[...]
    pad = jnp.zeros((nv, 4 * nv - 3 * nv - start.shape[1]), F32)
    pack_ref[0] = jnp.concatenate([gram[:, 2 * nv : 3 * nv], rim, inverse, start, pad], axis=1)
    basis_ref[...] = x2[H : H + cx, :, :, :cy]


def prolong(coefs, basis_ref, out_ref):
    k2, comps, cx, cy = out_ref.shape
    nv = basis_ref.shape[2]
    tiled = jnp.concatenate([coefs] * 8, axis=1)
    tiled = jnp.broadcast_to(tiled[:, None, :], (k2, 8, 8 * nv)).reshape(8 * k2, 8 * nv)
    same = lax.rem(iota(tiled.shape, 0), 8) == iota(tiled.shape, 1) // nv
    high, low = split(jnp.where(same, tiled, 0.0))
    for c in range(comps):
        for o in range(cx // 8):
            block = basis_ref[8 * o : 8 * o + 8, c].reshape(8 * nv, cy)
            bh, bl = split(block)
            out = dot(high, bh, NN) + (dot(low, bh, NN) + dot(high, bl, NN))
            out_ref[:, c, 8 * o : 8 * o + 8, :] = out.reshape(k2, 8, cy)


def level_kernel(spans, factor, p0, p1, p2, p3, basis_ref, out_ref, packs, z_ref):
    k2 = out_ref.shape[0]
    nv = basis_ref.shape[2]
    n = spans * nv
    s = lax.axis_index("sub")
    base = 0
    for part in (p0, p1, p2, p3):
        if base < spans:
            packs[base : base + part.shape[0]] = part[...]
            base += part.shape[0]
    lane = iota((nv, n), 1)
    upper, diagonal, starts = [], [], []
    for b in range(spans):
        block = packs[jnp.bitwise_xor(s, b)]
        zeros = jnp.zeros((nv, n - 4 * nv), F32)
        placed = jnp.concatenate([block, zeros], axis=1)
        pair = jnp.where(lane < nv, 0.5 * placed, jnp.where(lane < 2 * nv, placed, 0.0))
        upper.append(pltpu.roll(pair, nv * b, 1) if b else pair)
        inv = jnp.where((lane >= 2 * nv) & (lane < 3 * nv), placed, 0.0)
        diagonal.append(pltpu.roll(inv, (nv * (b - 2)) % n, 1) if b != 2 else inv)
        starts.append(block[:, 3 * nv : 3 * nv + k2])
    q = jnp.concatenate(upper, axis=0)
    inv = jnp.concatenate(diagonal, axis=0)
    y = jnp.concatenate(starts, axis=0)
    full = q + q.T
    u = dot3(y, inv, TN)
    z = dot3(dot3(u, full, NN), inv, NT)
    u = dot3(z, inv, NN)
    z = dot3(dot3(u, full, NN), inv, NT)
    gram = dot3(z, z, NT)
    gram = jnp.concatenate([gram, jnp.zeros((k2, 128 - k2), F32)], axis=1)
    solve = inverse_factor(gram, k2)[:, :k2]
    y = dot3(solve, z, NN)
    coefs = dot3(y, inv, NN)
    own = jnp.zeros((k2, nv), F32)
    for b in range(spans):
        own = jnp.where(s == b, coefs[:, nv * b : nv * b + nv], own)
    prolong(factor * own, basis_ref, out_ref)


def prolong_kernel(coefs_ref, basis_ref, out_ref):
    prolong(coefs_ref[...], basis_ref, out_ref)


def pairs(count, offset):
    return [q for i in range(offset, count - 1, 2) for q in ((i, i + 1), (i + 1, i))]


def from_behind(block, axis, distance):
    devices = range(lax.axis_size(axis))
    return lax.ppermute(block, axis, [(i - distance, i) for i in devices if i - distance in devices])


def level_coefs(pack, k2, factor):
    highest = lax.Precision.HIGHEST
    nv = pack.shape[0]
    own, rim, inv = pack[:, :nv], pack[:, nv : 2 * nv], pack[:, 2 * nv : 3 * nv]
    z = pack[:, 3 * nv : 3 * nv + k2]
    rim_prev = from_behind(rim, "sub", 1)
    for step in range(2):
        u = jnp.dot(inv.T, z, precision=highest)
        image = jnp.dot(own, u, precision=highest)
        image = image + jnp.dot(rim, from_behind(u, "sub", -1), precision=highest)
        image = image + jnp.dot(rim_prev.T, from_behind(u, "sub", 1), precision=highest)
        z = jnp.dot(inv, image, precision=highest)
    lower = jnp.linalg.cholesky(lax.psum(jnp.dot(z.T, z, precision=highest), "sub"))
    y = lax.linalg.triangular_solve(lower, z.T, left_side=True, lower=True)
    return factor * jnp.dot(y, inv, precision=highest)


def call(kernel, out_shape, scratch, name, in_specs=None):
    return pl.pallas_call(
        kernel,
        out_shape=out_shape,
        scratch_shapes=scratch,
        compiler_params=pltpu.CompilerParams(vmem_limit_bytes=48 * MIB),
        name=name,
        **({"in_specs": in_specs} if in_specs else {}),
    )


def on_device(start_vectors, stiffness, coupling, kept_ranks, level_start):
    spans, sects = lax.axis_size("sub"), lax.axis_size("sec")
    nv, comps, cx, cy = start_vectors.shape
    k2 = level_start.shape[1]
    channels = comps + 1
    xext, yext, wide = cx + 2 * H, cy + 2 * H, 2 * cy
    shape = jax.ShapeDtypeStruct
    vmem = pl.BlockSpec(memory_space=pltpu.VMEM)
    smem = pl.BlockSpec(memory_space=pltpu.SMEM)

    own, sec_out, sub_out = call(
        pack_kernel,
        (
            shape((cx, channels, nv, cy), BF16),
            shape((2, channels, nv, cy), BF16),
            shape((2, REACH, channels, nv, cy), BF16),
        ),
        [pltpu.VMEM((nv * comps * cx, cy), F32), pltpu.VMEM((8 * cx, cy), F32)],
        "pack",
    )(start_vectors, stiffness, coupling)
    sec_a = lax.ppermute(sec_out[0], "sec", pairs(sects, 0))
    sec_b = lax.ppermute(sec_out[1], "sec", pairs(sects, 1))
    edge = jnp.stack([sec_a, sec_b])
    sub_a = lax.ppermute(jnp.concatenate([sub_out[0], edge]), "sub", pairs(spans, 0))
    sub_b = lax.ppermute(jnp.concatenate([sub_out[1], edge]), "sub", pairs(spans, 1))

    def fine(*refs):
        fine_kernel((spans, sects), *refs)

    pack, basis = call(
        fine,
        (shape((1, nv, 4 * nv), F32), shape((cx, comps, nv, cy), F32)),
        [
            pltpu.VMEM((xext + 2, comps, nv, wide), F32),
            pltpu.VMEM((xext, comps, nv, wide), F32),
            pltpu.VMEM((xext, comps, nv, wide), F32),
            pltpu.VMEM((2 * H + 1, comps, nv, wide), F32),
            pltpu.VMEM((xext + 2, 8, wide), F32),
            pltpu.VMEM((2 * nv, 4 * nv), F32),
            pltpu.VMEM((2 * nv, 2 * nv), F32),
        ],
        "fine",
        [smem] + [vmem] * 6,
    )(kept_ranks, level_start, own, sec_a, sec_b, sub_a, sub_b)

    factor = math.sqrt(spans * comps * xext * yext)
    result = shape((k2, comps, cx, cy), F32)
    if spans != 8:
        return call(prolong_kernel, result, [], "prolong")(level_coefs(pack[0], k2, factor), basis)
    parts, held = [pack], pack
    for bit in (1, 2, 4):
        parts.append(lax.ppermute(held, "sub", [(i, i ^ bit) for i in range(spans)]))
        held = jnp.concatenate([held, parts[-1]])

    def level(*refs):
        level_kernel(spans, factor, *refs)

    return call(
        level, result, [pltpu.VMEM((spans, nv, 4 * nv), F32), pltpu.VMEM((k2, spans * nv), F32)], "level"
    )(*parts, basis)


def solution(mesh):
    placed = (
        P(None, None, "sub", "sec"),
        P(None, "sub", "sec"),
        P("sub", "sec"),
        P("sub", "sec"),
        P("sub", None),
    )
    return jax.shard_map(
        on_device,
        mesh=mesh,
        in_specs=placed,
        out_specs=P(None, None, "sub", "sec"),
        check_vma=False,
    )
```

```python
import math

import jax
import jax.numpy as jnp
from jax import lax
from jax.experimental import pallas as pl
from jax.experimental.pallas import tpu as pltpu
from jax.sharding import PartitionSpec as P

H = 4
MIB = 1 << 20
F32 = jnp.float32
BF16 = jnp.bfloat16
NN = (((1,), (0,)), ((), ()))
NT = (((1,), (1,)), ((), ()))
TN = (((0,), (0,)), ((), ()))


def iota(shape, dim):
    return lax.broadcasted_iota(jnp.int32, shape, dim)


def split(x):
    high = x.astype(BF16)
    return high, (x - high.astype(F32)).astype(BF16)


def dot(a, b, dims):
    return lax.dot_general(a, b, dims, preferred_element_type=F32)


def dot3(a, b, dims):
    (ah, al), (bh, bl) = split(a), split(b)
    return dot(ah, bh, dims) + (dot(ah, bl, dims) + dot(al, bh, dims))


def inverse_factor(gram, size):
    row, lane = iota((size, 128), 0), iota((size, 128), 1)
    work = jnp.where(lane < size, gram, jnp.where(lane == row + size, 1.0, 0.0))
    for j in range(size - 1):
        column = work[:, j : j + 1]
        pivot = work[j : j + 1, :]
        factor = jnp.where(iota((size, 1), 0) > j, column / column[j : j + 1, :], 0.0)
        work = work - factor * pivot
    diag = jnp.sum(jnp.where(lane == row, work, 0.0), axis=1, keepdims=True)
    return pltpu.roll(work / jnp.sqrt(diag), 128 - size, 1)


def slots_of(cx):
    own = cx // H
    return own, own, own + 1, own + 2, own + 3


def halves(octet_a, octet_b):
    return jnp.where(iota(octet_a.shape, 0) < H, octet_a, octet_b)


def swap(octet):
    return pltpu.roll(octet, H, 0)


def pack_kernel(v_hbm, k_hbm, g_hbm, own_ref, kt_ref, sec_a, sec_b, v_buf, k_buf, g_buf, vf, kf, sems):
    nv, comps, cx, cy = v_buf.shape
    copies = [
        pltpu.make_async_copy(src, dst, sems.at[i])
        for i, (src, dst) in enumerate(((k_hbm, k_buf), (g_hbm, g_buf), (v_hbm, v_buf)))
    ]
    for copy in copies:
        copy.start()
    sec_even = lax.rem(lax.axis_index("sec"), 2) == 0
    for copy in copies:
        copy.wait()
    vf[...] = v_buf[...].astype(F32).reshape(vf.shape)
    kf[: comps * cx] = k_buf[...].astype(F32).reshape(comps * cx, cy)
    kf[comps * cx :] = g_buf[...].astype(F32)
    firsts, lasts = [], []
    own = cx // H
    for p in range(own + 2):
        rows = [b * own + p for b in range(H)] if p < own else [b + (p - own) * (cx - H) for b in range(H)]
        for c in range(comps):
            stack = [vf[pl.ds(c * cx + x, nv, stride=comps * cx), :] for x in rows]
            turned = jnp.concatenate(stack, axis=0).T
            own_ref[p, c] = turned.astype(BF16)
            firsts.append(turned[:8])
            lasts.append(turned[cy - 8 :])
    turned = kf[...].T
    kt_ref[...] = turned.astype(BF16)
    for octets, value in ((firsts, turned[:8]), (lasts, turned[cy - 8 :])):
        octets.append(value)
        if len(octets) % 2:
            octets.append(jnp.zeros_like(value))
    pairs_of = range(0, len(firsts), 2)
    left = [halves(firsts[q], swap(firsts[q + 1])) for q in pairs_of]
    right = [halves(swap(lasts[q]), lasts[q + 1]) for q in pairs_of]
    left, right = jnp.concatenate(left, axis=0), jnp.concatenate(right, axis=0)
    sec_a[...] = jnp.where(sec_even, right, left).astype(BF16)
    sec_b[...] = jnp.where(sec_even, left, right).astype(BF16)


def margin_octets(sec_a, sec_b, sec_even, count):
    a, b = sec_a[...].astype(F32), sec_b[...].astype(F32)
    hi, lo = jnp.where(sec_even, a, b), jnp.where(sec_even, b, a)
    out = []
    for q in range(count):
        at = slice(8 * (q // 2), 8 * (q // 2) + 8)
        out.append(halves(swap(hi[at]), lo[at]) if q % 2 else halves(hi[at], swap(lo[at])))
    return out


def edge_kernel(own_ref, kt_ref, sec_a, sec_b, sub_a, sub_b):
    slots, comps, cy, lanes = own_ref.shape
    sub_even = lax.rem(lax.axis_index("sub"), 2) == 0
    sec_even = lax.rem(lax.axis_index("sec"), 2) == 0
    octets = margin_octets(sec_a, sec_b, sec_even, slots * comps + 1)
    first, last = slots - 2, slots - 1
    head = octets[first * comps : first * comps + comps] + octets[-1:]
    tail = octets[last * comps : last * comps + comps] + octets[-1:]
    head, tail = jnp.concatenate(head, axis=0), jnp.concatenate(tail, axis=0)
    for ref, to_next in ((sub_a, sub_even), (sub_b, jnp.logical_not(sub_even))):
        slot = jnp.where(to_next, last, first)
        for c in range(comps):
            ref[c * cy : (c + 1) * cy] = own_ref[slot, c]
        ref[comps * cy : (comps + 1) * cy] = kt_ref[...]
        ref[(comps + 1) * cy :] = jnp.where(to_next, tail, head).astype(BF16)


def fine_kernel(sizes, rank_ref, start_ref, own_ref, kt_ref, sec_a, sec_b, sub_a, sub_b, pack_ref, x2, v0, x1, coef, high2, low2, high3, low3, margin3):
    spans, sects = sizes
    _, comps, cy, lanes = own_ref.shape
    nv = start_ref.shape[0]
    cx = kt_ref.shape[1] // (comps + 1)
    OWN, BEFORE, AFTER, HEAD, TAIL = slots_of(cx)
    s, t = lax.axis_index("sub"), lax.axis_index("sec")
    sub_even, sec_even = lax.rem(s, 2) == 0, lax.rem(t, 2) == 0
    kinds = comps + 1
    low, top = slice(0, 8), slice(8 + cy, 16 + cy)
    mid = slice(8, 8 + cy)

    octets = margin_octets(sec_a, sec_b, sec_even, (OWN + 2) * comps + 1)

    def put(slot, c, rows, octet):
        v0[slot, c, mid, :] = rows
        v0[slot, c, low, :] = octet
        v0[slot, c, top, :] = octet

    for p in range(OWN + 2):
        for c in range(comps):
            put(p if p < OWN else HEAD + p - OWN, c, own_ref[p, c].astype(F32), octets[p * comps + c])

    def received(first, count):
        a, b = sub_a[first : first + count].astype(F32), sub_b[first : first + count].astype(F32)
        return jnp.where(sub_even, a, b), jnp.where(sub_even, b, a)

    for c in range(comps):
        after, before = received(c * cy, cy)
        after_octet, before_octet = received(kinds * cy + 8 * c, 8)
        put(BEFORE, c, before, before_octet)
        put(AFTER, c, after, after_octet)

    octet_row = iota((8, lanes), 0)
    col_in = jnp.where(octet_row < H, jnp.where(t < sects - 1, 1.0, 0.0), jnp.where(t > 0, 1.0, 0.0))
    has_before, has_after = jnp.where(s > 0, 1.0, 0.0), jnp.where(s < spans - 1, 1.0, 0.0)
    row_in = {BEFORE: has_before, AFTER: has_after}

    def padded(rows, octet):
        return jnp.concatenate([rows, octet, jnp.zeros_like(octet)], axis=0).astype(BF16)

    after, before = received(comps * cy, cy)
    after_octet, before_octet = received(kinds * cy + 8 * comps, 8)
    table = padded(kt_ref[...].astype(F32), octets[-1])
    table_after, table_before = padded(after, after_octet), padded(before, before_octet)
    table_first = jnp.concatenate([table, table_after], axis=0)
    table_last = jnp.concatenate([table, table_before], axis=0)
    source, block = iota((lanes, lanes), 0), iota((lanes, lanes), 1) // nv

    def spread(table, wanted):
        pick = [jnp.where(source == kind * cx + wanted, 1.0, 0.0).astype(BF16) for kind in range(kinds)]
        out = dot(table, jnp.concatenate(pick, axis=1), NN)
        return [out[:, kind * lanes : (kind + 1) * lanes] for kind in range(kinds)]

    def put_coef(slot, values, first):
        inside = row_in.get(slot)
        for at, length, mask in ((0, cy, inside), (cy, 8, col_in if inside is None else col_in * inside)):
            rows = [v[first + at : first + at + length] for v in values]
            for kind in range(kinds):
                value = 4.0 + rows[kind] - rows[comps] if kind < comps else rows[kind]
                coef[slot, kind, at : at + length, :] = value if mask is None else value * mask

    for p in range(OWN):
        put_coef(p, spread(table, block * OWN + p), 0)
    values = spread(table_first, block)
    put_coef(HEAD, values, 0)
    put_coef(AFTER, values, cy + 16)
    values = spread(table_last, block + (cx - H))
    put_coef(TAIL, values, 0)
    put_coef(BEFORE, values, cy + 16)

    def operator(src, rows, first_row, length, shifted, strips, emit):
        lane = iota((length, lanes), 1)
        in_first, in_last = lane < nv, lane >= lanes - nv
        masked = shifted is not None

        def at(slot, c):
            return src[slot, c, rows(0), :]

        def up_of(slot, c):
            if 0 < slot < OWN:
                return at(slot - 1, c)
            if slot in (0, AFTER):
                return pltpu.roll(jnp.where(in_last, at(BEFORE if slot == 0 else OWN - 1, c), at(OWN - 1 if slot == 0 else AFTER, c)), nv, 1)
            if slot == HEAD:
                return pltpu.roll(jnp.where(in_last, at(BEFORE, c), at(HEAD, c)), nv, 1)
            return jnp.where(in_first, 0.0, pltpu.roll(at(slot, c), nv, 1))

        def down_of(slot, c):
            if slot < OWN - 1:
                return at(slot + 1, c)
            if slot in (OWN - 1, BEFORE):
                return pltpu.roll(jnp.where(in_first, at(AFTER if slot == OWN - 1 else 0, c), at(0 if slot == OWN - 1 else BEFORE, c)), lanes - nv, 1)
            if slot == TAIL:
                return pltpu.roll(jnp.where(in_first, at(AFTER, c), at(TAIL, c)), lanes - nv, 1)
            return jnp.where(in_last, 0.0, pltpu.roll(at(slot, c), lanes - nv, 1))

        for slot in range(TAIL + 1 if strips else AFTER + 1):
            v = [at(slot, c) for c in range(comps)]
            weight = [coef[slot, kind, first_row, :] for kind in range(kinds)]
            total = weight[comps] * (v[0] + v[1] + v[2])
            for c in range(comps):
                if masked:
                    sides = shifted(slot, c)
                else:
                    sides = src[slot, c, rows(-1), :] + src[slot, c, rows(1), :]
                beside = sides + (up_of(slot, c) + down_of(slot, c))
                inside = row_in.get(slot)
                if masked:
                    beside = beside * (col_in if inside is None else col_in * inside)
                elif inside is not None:
                    beside = beside * inside
                emit(slot, c, weight[c] * v[c] + total - beside)

    def apply(src, strips, emit_rows, emit_margin):
        def body(j, carry):
            base = 16 * j

            def rows(d):
                start = 8 + base + d
                return pl.ds(pl.multiple_of(start, 8) if d == 0 else start, 16)

            def emit(slot, c, value):
                emit_rows(slot, c, pl.multiple_of(base, 16), value)

            operator(src, rows, pl.ds(pl.multiple_of(base, 16), 16), 16, None, strips, emit)
            return carry

        lax.fori_loop(0, cy // 16, body, 0)

        def shifted(slot, c):
            left = jnp.where(octet_row == H, 0.0, src[slot, c, 7 + cy : 15 + cy, :])
            return left + jnp.where(octet_row == H - 1, 0.0, src[slot, c, 1:9, :])

        operator(src, lambda d: top, slice(cy, cy + 8), 8, shifted, strips, emit_margin)

    def store(dst, split_too=False):
        def emit_rows(slot, c, base, value):
            dst[slot, c, pl.ds(base + 8, 16), :] = value
            if split_too and slot < HEAD:
                high2[slot, c, pl.ds(base, 16), :], low2[slot, c, pl.ds(base, 16), :] = split(value)

        def emit_margin(slot, c, value):
            dst[slot, c, low, :] = value
            dst[slot, c, top, :] = value

        return emit_rows, emit_margin

    apply(v0, True, *store(x1))
    apply(x1, True, *store(x2, True))

    def split_rows(slot, c, base, value):
        high3[slot, c, pl.ds(base, 16), :], low3[slot, c, pl.ds(base, 16), :] = split(value)

    def keep_margin(slot, c, value):
        margin3[slot, c] = value

    apply(x2, False, split_rows, keep_margin)

    def fold(z):
        return sum(pltpu.roll(z[b * nv : (b + 1) * nv], (z.shape[1] - b * nv) % z.shape[1], 1) if b else z[:nv] for b in range(H))

    def gram_of(h2, l2, h3, l3):
        main = dot(h2, jnp.concatenate([h2, l2, h3, l3], axis=1), TN)
        return main, dot(l2, h3, TN)

    def flat(ref, first, count):
        return ref[first : first + count].reshape(count * comps * cy, lanes)

    octet_margins = [x2[slot, c, top, :] for slot in range(AFTER + 1) for c in range(comps)]
    h2, l2 = split(jnp.concatenate(octet_margins, axis=0))
    h3, l3 = split(margin3[...].reshape((AFTER + 1) * comps * 8, lanes))
    main, cross = gram_of(h2, l2, h3, l3)
    for first in range(0, AFTER + 1, 2):
        part = gram_of(*(flat(ref, first, 2) for ref in (high2, low2, high3, low3)))
        main, cross = main + part[0], cross + part[1]
    main, cross = fold(main), fold(cross)[:, :nv]
    mixed = main[:, lanes : lanes + nv]
    gram = main[:, :nv] + (mixed + mixed.T)
    image = main[:, 2 * lanes : 2 * lanes + nv] + main[:, 3 * lanes : 3 * lanes + nv] + cross

    def rim(strip, first, block, own_first):
        own, other = [], []
        for at, weight_at in ((mid, slice(0, cy)), (top, slice(cy, cy + 8))):
            for c in range(comps):
                held = [x2[first + i, c, at, block * nv : (block + 1) * nv] for i in range(H)]
                weight = coef[strip, c, weight_at, :] + coef[strip, comps, weight_at, :]
                own.append(jnp.concatenate(held, axis=1) * weight)
                other.append(x2[strip, c, at, :])
        own.append(jnp.zeros((8, lanes), F32))
        other.append(jnp.zeros((8, lanes), F32))
        own, other = jnp.concatenate(own, axis=0), jnp.concatenate(other, axis=0)
        a, b = (own, other) if own_first else (other, own)
        return fold(dot3(a, b, TN))[:, :nv]

    rim_next = rim(TAIL, OWN - H, H - 1, True) * has_after
    rim_prev = rim(HEAD, 0, 0, False) * has_before

    pad = jnp.zeros((nv, lanes - nv), F32)
    inverse = inverse_factor(jnp.concatenate([gram, pad], axis=1), nv)[:, :nv]
    inverse = jnp.where(iota((nv, nv), 0) < rank_ref[0, 0], inverse, 0.0)
    pack_ref[0, :nv] = jnp.concatenate([image, rim_next, rim_prev, inverse], axis=1)
    start = [start_ref[8 * i : 8 * i + 8, :] for i in range(nv // 8)]
    pad = jnp.zeros((8, lanes - start_ref.shape[1] * len(start)), F32)
    pack_ref[0, nv:] = jnp.concatenate(start + [pad], axis=1)


def prolong(coefs, basis_ref, out_ref):
    k2, comps, cx, cy = out_ref.shape
    nv = coefs.shape[1]
    own = cx // H
    tiled = jnp.concatenate([coefs] * H, axis=1)
    tiled = jnp.concatenate([tiled, jnp.zeros_like(tiled)], axis=1)[:, : H * nv]
    tiled = jnp.broadcast_to(tiled[:, None, :], (k2, 8, H * nv)).reshape(8 * k2, H * nv)
    same = lax.rem(iota(tiled.shape, 0), 8) == iota(tiled.shape, 1) // nv
    high, low = split(jnp.where(same, tiled, 0.0))
    left = jnp.concatenate([high, low, high], axis=1)
    for c in range(comps):
        for p in range(own):
            bh, bl = split(basis_ref[p, c, 8 : 8 + cy, :])
            out = dot(left, jnp.concatenate([bh, bh, bl], axis=1), NT).reshape(k2, 8, cy)
            out_ref[:, c, pl.ds(p, H, stride=own), :] = out[:, :H]


def starts_of(block, nv, k2):
    return jnp.concatenate([block[nv:, k2 * i : k2 * i + k2] for i in range(nv // 8)], axis=0)


def level_kernel(spans, nv, factor, p0, p1, p2, p3, basis_ref, out_ref, packs):
    k2 = out_ref.shape[0]
    n = spans * nv
    s = lax.axis_index("sub")
    base = 0
    for part in (p0, p1, p2, p3):
        packs[base : base + part.shape[0]] = part[...]
        base += part.shape[0]
    lane = iota((nv, n), 1)
    upper, diagonal, starts = [], [], []
    blocks = [packs[jnp.bitwise_xor(s, b)] for b in range(spans)]
    zeros = jnp.zeros((nv, n - 4 * nv), F32)
    for b in range(spans):
        placed = jnp.concatenate([blocks[b][:nv], zeros], axis=1)
        pair = jnp.where(lane < nv, 0.5 * placed, jnp.where(lane < 2 * nv, placed, 0.0))
        if b + 1 < spans:
            after = jnp.concatenate([blocks[b + 1][:nv], zeros], axis=1)
            pair = pair + pltpu.roll(jnp.where((lane >= 2 * nv) & (lane < 3 * nv), after, 0.0), n - nv, 1)
        upper.append(pltpu.roll(pair, nv * b, 1) if b else pair)
        inv = jnp.where((lane >= 3 * nv) & (lane < 4 * nv), placed, 0.0)
        diagonal.append(pltpu.roll(inv, (nv * (b - 3)) % n, 1) if b != 3 else inv)
        starts.append(starts_of(blocks[b], nv, k2))
    q = jnp.concatenate(upper, axis=0)
    inv = jnp.concatenate(diagonal, axis=0)
    y = jnp.concatenate(starts, axis=0)
    full = q + q.T
    u = dot3(y, inv, TN)
    z = dot3(dot3(u, full, NN), inv, NT)
    u = dot3(z, inv, NN)
    z = dot3(dot3(u, full, NN), inv, NT)
    gram = dot3(z, z, NT)
    gram = jnp.concatenate([gram, jnp.zeros((k2, 128 - k2), F32)], axis=1)
    solve = inverse_factor(gram, k2)[:, :k2]
    y = dot3(solve, z, NN)
    coefs = dot3(y, inv, NN)
    own = jnp.zeros((k2, nv), F32)
    for b in range(spans):
        own = jnp.where(s == b, coefs[:, nv * b : nv * b + nv], own)
    prolong(factor * own, basis_ref, out_ref)


def pairs(count, offset):
    return [q for i in range(offset, count - 1, 2) for q in ((i, i + 1), (i + 1, i))]


def from_behind(block, axis, distance):
    devices = range(lax.axis_size(axis))
    return lax.ppermute(block, axis, [(i - distance, i) for i in devices if i - distance in devices])


def level_coefs(pack, nv, k2, factor):
    highest = lax.Precision.HIGHEST
    own, rim_next, rim_prev, inv = (pack[:nv, nv * i : nv * i + nv] for i in range(4))
    z = starts_of(pack, nv, k2)
    rim = rim_next + from_behind(rim_prev, "sub", -1)
    rim_before = from_behind(rim, "sub", 1)
    for step in range(2):
        u = jnp.dot(inv.T, z, precision=highest)
        image = jnp.dot(own, u, precision=highest)
        image = image + jnp.dot(rim, from_behind(u, "sub", -1), precision=highest)
        image = image + jnp.dot(rim_before.T, from_behind(u, "sub", 1), precision=highest)
        z = jnp.dot(inv, image, precision=highest)
    lower = jnp.linalg.cholesky(lax.psum(jnp.dot(z.T, z, precision=highest), "sub"))
    y = lax.linalg.triangular_solve(lower, z.T, left_side=True, lower=True)
    return factor * jnp.dot(y, inv, precision=highest)


def call(kernel, out_shape, scratch, name, in_specs=None):
    return pl.pallas_call(
        kernel,
        out_shape=out_shape,
        scratch_shapes=scratch,
        compiler_params=pltpu.CompilerParams(vmem_limit_bytes=48 * MIB),
        name=name,
        **({"in_specs": in_specs} if in_specs else {}),
    )


def on_device(start_vectors, stiffness, coupling, kept_ranks, level_start):
    spans, sects = lax.axis_size("sub"), lax.axis_size("sec")
    nv, comps, cx, cy = start_vectors.shape
    k2 = level_start.shape[1]
    channels = comps + 1
    slots = slots_of(cx)[-1] + 1
    shape = jax.ShapeDtypeStruct
    vmem = pl.BlockSpec(memory_space=pltpu.VMEM)
    smem = pl.BlockSpec(memory_space=pltpu.SMEM)
    hbm = pl.BlockSpec(memory_space=pltpu.HBM)

    pieces = (cx // H + 2) * comps + 1
    sec_shape = shape((-(-pieces // 2) * 8, cy), BF16)
    own, kt, sec_a, sec_b = call(
        pack_kernel,
        (shape((cx // H + 2, comps, cy, H * nv), BF16), shape((cy, channels * cx), BF16), sec_shape, sec_shape),
        [
            pltpu.VMEM(start_vectors.shape, BF16),
            pltpu.VMEM(stiffness.shape, BF16),
            pltpu.VMEM(coupling.shape, BF16),
            pltpu.VMEM((nv * comps * cx, cy), F32),
            pltpu.VMEM((channels * cx, cy), F32),
            pltpu.SemaphoreType.DMA((3,)),
        ],
        "pack",
        [hbm] * 3,
    )(start_vectors, stiffness, coupling)
    sec_a = lax.ppermute(sec_a, "sec", pairs(sects, 0))
    sec_b = lax.ppermute(sec_b, "sec", pairs(sects, 1))
    sub_shape = shape((channels * (cy + 8), H * nv), BF16)
    sub_a, sub_b = call(edge_kernel, (sub_shape, sub_shape), [], "edge")(own, kt, sec_a, sec_b)
    sub_a = lax.ppermute(sub_a, "sub", pairs(spans, 0))
    sub_b = lax.ppermute(sub_b, "sub", pairs(spans, 1))

    def fine(*refs):
        fine_kernel((spans, sects), *refs)

    rows = (slots, comps, cy + 16, H * nv)
    halved = pltpu.VMEM((slots - 2, comps, cy, H * nv), BF16)
    pack, basis = call(
        fine,
        (shape((1, nv + 8, cy), F32), shape(rows, F32)),
        [
            pltpu.VMEM(rows, F32),
            pltpu.VMEM(rows, F32),
            pltpu.VMEM((slots, channels, cy + 8, H * nv), F32),
            halved,
            halved,
            halved,
            halved,
            pltpu.VMEM((slots - 2, comps, 8, H * nv), F32),
        ],
        "fine",
        [smem] + [vmem] * 7,
    )(kept_ranks, level_start, own, kt, sec_a, sec_b, sub_a, sub_b)

    factor = math.sqrt(spans * comps * (cx + 2 * H) * (cy + 2 * H))
    result = shape((k2, comps, cx, cy), F32)
    if spans != 8:

        def prolong_kernel(coefs_ref, basis_ref, out_ref):
            prolong(coefs_ref[...], basis_ref, out_ref)

        return call(prolong_kernel, result, [], "prolong")(level_coefs(pack[0], nv, k2, factor), basis)
    parts, held = [pack], pack
    for bit in (1, 2, 4):
        parts.append(lax.ppermute(held, "sub", [(i, i ^ bit) for i in range(spans)]))
        held = jnp.concatenate([held, parts[-1]])

    def level(*refs):
        level_kernel(spans, nv, factor, *refs)

    return call(level, result, [pltpu.VMEM((spans,) + pack.shape[1:], F32)], "level")(*parts, basis)


def solution(mesh):
    placed = (
        P(None, None, "sub", "sec"),
        P(None, "sub", "sec"),
        P("sub", "sec"),
        P("sub", "sec"),
        P("sub", None),
    )
    return jax.shard_map(
        on_device,
        mesh=mesh,
        in_specs=placed,
        out_specs=P(None, None, "sub", "sec"),
        check_vma=False,
    )
```

```python
import math

import jax
import jax.numpy as jnp
from jax import lax
from jax.experimental import pallas as pl
from jax.experimental.pallas import tpu as pltpu
from jax.sharding import PartitionSpec as P

H = 4
MIB = 1 << 20
VMEM_MIB = 24
F32 = jnp.float32
BF16 = jnp.bfloat16
NN = (((1,), (0,)), ((), ()))
NT = (((1,), (1,)), ((), ()))
TN = (((0,), (0,)), ((), ()))


def iota(shape, dim):
    return lax.broadcasted_iota(jnp.int32, shape, dim)


def split(x):
    high = x.astype(BF16)
    return high, (x - high.astype(F32)).astype(BF16)


def dot(a, b, dims):
    return lax.dot_general(a, b, dims, preferred_element_type=F32)


def dot3(a, b, dims):
    (ah, al), (bh, bl) = split(a), split(b)
    return dot(ah, bh, dims) + (dot(ah, bl, dims) + dot(al, bh, dims))


def inverse_factor(gram, size, step=4):
    row, lane = iota((size, 128), 0), iota((size, 128), 1)
    work = jnp.where(lane < size, gram, jnp.where(lane == row + size, 1.0, 0.0))
    for first in range(0, size, step):
        columns = [jnp.broadcast_to(work[:, j : j + 1], (size, 128)) for j in range(first, first + step)]
        update = None
        for i, j in enumerate(range(first, min(first + step, size - 1))):
            factor = jnp.where(row > j, columns[i] / columns[i][j : j + 1, :], 0.0)
            for later in range(i + 1, step):
                columns[later] = columns[later] - factor * columns[later][j : j + 1, :]
            pivot = work[j : j + 1, :]
            if update is not None:
                pivot = pivot - update[j : j + 1, :]
            update = factor * pivot if update is None else update + factor * pivot
        work = work - update
    diag = jnp.sum(jnp.where(lane == row, work, 0.0), axis=1, keepdims=True)
    return pltpu.roll(work / jnp.sqrt(diag), 128 - size, 1)


def slots_of(cx):
    own = cx // H
    return own, own, own + 1, own + 2, own + 3


def halves(octet_a, octet_b):
    return jnp.where(iota(octet_a.shape, 0) < H, octet_a, octet_b)


def swap(octet):
    return pltpu.roll(octet, H, 0)


def pack_kernel(
    v_hbm, k_hbm, g_hbm, start_hbm, own_ref, kt_ref, sec_a, sec_b, start_ref, v_buf, k_buf, g_buf, vf, kf, sems
):
    comps, nv, cx, cy = v_buf.shape
    copies = [pltpu.make_async_copy(v_hbm.at[:, c], v_buf.at[c], sems.at[c]) for c in range(comps)]
    copies.append(pltpu.make_async_copy(k_hbm, k_buf, sems.at[comps]))
    copies.append(pltpu.make_async_copy(g_hbm, g_buf, sems.at[comps + 1]))
    copies.append(pltpu.make_async_copy(start_hbm, start_ref, sems.at[comps + 2]))
    for copy in copies:
        copy.start()
    sec_even = lax.rem(lax.axis_index("sec"), 2) == 0
    own = cx // H
    pieces = (own + 2) * comps + 1
    firsts, lasts = [None] * pieces, [None] * pieces
    for c in range(comps):
        copies[c].wait()
        vf[c] = v_buf[c].astype(F32).reshape(nv * cx, cy)
        for p in range(own + 2):
            rows = [b * own + p for b in range(H)] if p < own else [b + (p - own) * (cx - H) for b in range(H)]
            stack = [vf[c, pl.ds(x, nv, stride=cx), :] for x in rows]
            turned = jnp.concatenate(stack, axis=0).T
            own_ref[p, c] = turned.astype(BF16)
            firsts[p * comps + c], lasts[p * comps + c] = turned[:8], turned[cy - 8 :]
    for copy in copies[comps:]:
        copy.wait()
    kf[: comps * cx] = k_buf[...].astype(F32).reshape(comps * cx, cy)
    kf[comps * cx :] = g_buf[...].astype(F32)
    turned = kf[...].T
    kt_ref[...] = turned.astype(BF16)
    firsts[-1], lasts[-1] = turned[:8], turned[cy - 8 :]
    for octets in (firsts, lasts):
        if len(octets) % 2:
            octets.append(jnp.zeros((8, cy), F32))
    pairs_of = range(0, len(firsts), 2)
    left = [halves(firsts[q], swap(firsts[q + 1])) for q in pairs_of]
    right = [halves(swap(lasts[q]), lasts[q + 1]) for q in pairs_of]
    left, right = jnp.concatenate(left, axis=0), jnp.concatenate(right, axis=0)
    sec_a[...] = jnp.where(sec_even, right, left).astype(BF16)
    sec_b[...] = jnp.where(sec_even, left, right).astype(BF16)


def margin_octets(sec_a, sec_b, sec_even, count):
    a, b = sec_a[...].astype(F32), sec_b[...].astype(F32)
    hi, lo = jnp.where(sec_even, a, b), jnp.where(sec_even, b, a)
    out = []
    for q in range(count):
        at = slice(8 * (q // 2), 8 * (q // 2) + 8)
        out.append(halves(swap(hi[at]), lo[at]) if q % 2 else halves(hi[at], swap(lo[at])))
    return out


def edge_kernel(own_ref, kt_ref, sec_a, sec_b, sub_a, sub_b):
    slots, comps, cy, lanes = own_ref.shape
    sub_even = lax.rem(lax.axis_index("sub"), 2) == 0
    sec_even = lax.rem(lax.axis_index("sec"), 2) == 0
    octets = margin_octets(sec_a, sec_b, sec_even, slots * comps + 1)
    first, last = slots - 2, slots - 1
    head = octets[first * comps : first * comps + comps] + octets[-1:]
    tail = octets[last * comps : last * comps + comps] + octets[-1:]
    head, tail = jnp.concatenate(head, axis=0), jnp.concatenate(tail, axis=0)
    for ref, to_next in ((sub_a, sub_even), (sub_b, jnp.logical_not(sub_even))):
        slot = jnp.where(to_next, last, first)
        for c in range(comps):
            ref[c * cy : (c + 1) * cy] = own_ref[slot, c]
        ref[comps * cy : (comps + 1) * cy] = kt_ref[...]
        ref[(comps + 1) * cy :] = jnp.where(to_next, tail, head).astype(BF16)


def spread(table, wanted, kinds, cx):
    lanes = table.shape[1]
    source = iota((lanes, lanes), 0)
    pick = [jnp.where(source == kind * cx + wanted, 1.0, 0.0).astype(BF16) for kind in range(kinds)]
    out = dot(table, jnp.concatenate(pick, axis=1), NN)
    return [out[:, kind * lanes : (kind + 1) * lanes] for kind in range(kinds)]


def terms_of(rows):
    return [4.0 + k - rows[-1] for k in rows[:-1]] + [rows[-1]]


def row_of_slot(p, own, cx, block):
    return block * own + p if p < own else block + (p - own) * (cx - H)


def prep_kernel(own_ref, kt_ref, v0, coef):
    slots, comps, cy, lanes = own_ref.shape
    own, kinds = slots - 2, comps + 1
    cx = kt_ref.shape[1] // kinds
    head = slots_of(cx)[3]
    block = iota((lanes, lanes), 1) // (lanes // H)
    for p in range(slots):
        slot = p if p < own else head + p - own
        for c in range(comps):
            v0[slot, c, 8 : 8 + cy, :] = own_ref[p, c].astype(F32)
        values = spread(kt_ref[...], row_of_slot(p, own, cx, block), kinds, cx)
        for kind, value in enumerate(terms_of(values)):
            coef[slot, kind, :cy, :] = value


def fine_kernel(sizes, rank_ref, start_ref, v0_in, coef_in, kt_ref, sec_a, sec_b, sub_a, sub_b, pack_ref, high2, low2, v0, coef, x1, x2, high3, low3, margin3):
    spans, sects = sizes
    _, comps, cy, lanes = high2.shape
    nv = start_ref.shape[1]
    cx = kt_ref.shape[1] // (comps + 1)
    OWN, BEFORE, AFTER, HEAD, TAIL = slots_of(cx)
    s, t = lax.axis_index("sub"), lax.axis_index("sec")
    sub_even, sec_even = lax.rem(s, 2) == 0, lax.rem(t, 2) == 0
    kinds = comps + 1
    low, top = slice(0, 8), slice(8 + cy, 16 + cy)
    mid = slice(8, 8 + cy)
    octets = margin_octets(sec_a, sec_b, sec_even, (OWN + 2) * comps + 1)

    def put_octet(slot, c, octet):
        v0[slot, c, low, :] = octet
        v0[slot, c, top, :] = octet

    def received(first, count):
        a, b = sub_a[first : first + count].astype(F32), sub_b[first : first + count].astype(F32)
        return jnp.where(sub_even, a, b), jnp.where(sub_even, b, a)

    for c in range(comps):
        for p in range(OWN + 2):
            put_octet(p if p < OWN else HEAD + p - OWN, c, octets[p * comps + c])
        v0[AFTER, c, mid, :], v0[BEFORE, c, mid, :] = received(c * cy, cy)
        after_octet, before_octet = received(kinds * cy + 8 * c, 8)
        put_octet(BEFORE, c, before_octet)
        put_octet(AFTER, c, after_octet)

    octet_row = iota((8, lanes), 0)
    col_in = jnp.where(octet_row < H, jnp.where(t < sects - 1, 1.0, 0.0), jnp.where(t > 0, 1.0, 0.0))
    has_before, has_after = jnp.where(s > 0, 1.0, 0.0), jnp.where(s < spans - 1, 1.0, 0.0)
    row_in = {BEFORE: has_before, AFTER: has_after}
    octet_block = iota((8, lanes), 1) // nv
    for p in range(OWN + 2):
        slot = p if p < OWN else HEAD + p - OWN
        wanted = row_of_slot(p, OWN, cx, octet_block)
        rows = [jnp.take_along_axis(octets[-1], wanted + kind * cx, axis=1) for kind in range(kinds)]
        for kind, value in enumerate(terms_of(rows)):
            coef[slot, kind, cy : cy + 8, :] = value * col_in
    after, before = received(comps * cy, cy)
    after_octet, before_octet = received(kinds * cy + 8 * comps, 8)
    block = iota((lanes, lanes), 1) // nv
    for slot, rows, octet, p in ((AFTER, after, after_octet, OWN), (BEFORE, before, before_octet, OWN + 1)):
        table = jnp.concatenate([rows, octet, jnp.zeros_like(octet)], axis=0).astype(BF16)
        values = spread(table, row_of_slot(p, OWN, cx, block), kinds, cx)
        for kind, value in enumerate(terms_of(values)):
            coef[slot, kind, :cy, :] = value[:cy] * row_in[slot]
            coef[slot, kind, cy : cy + 8, :] = value[cy : cy + 8] * (col_in * row_in[slot])

    def operator(src, rows, first_row, length, shifted, strips, emit):
        lane = iota((length, lanes), 1)
        in_first, in_last = lane < nv, lane >= lanes - nv
        masked = shifted is not None

        def at(slot, c):
            return src[slot, c, rows(0), :]

        def up_of(slot, c):
            if 0 < slot < OWN:
                return at(slot - 1, c)
            if slot in (0, AFTER):
                return pltpu.roll(jnp.where(in_last, at(BEFORE if slot == 0 else OWN - 1, c), at(OWN - 1 if slot == 0 else AFTER, c)), nv, 1)
            if slot == HEAD:
                return pltpu.roll(jnp.where(in_last, at(BEFORE, c), at(HEAD, c)), nv, 1)
            return jnp.where(in_first, 0.0, pltpu.roll(at(slot, c), nv, 1))

        def down_of(slot, c):
            if slot < OWN - 1:
                return at(slot + 1, c)
            if slot in (OWN - 1, BEFORE):
                return pltpu.roll(jnp.where(in_first, at(AFTER if slot == OWN - 1 else 0, c), at(0 if slot == OWN - 1 else BEFORE, c)), lanes - nv, 1)
            if slot == TAIL:
                return pltpu.roll(jnp.where(in_first, at(AFTER, c), at(TAIL, c)), lanes - nv, 1)
            return jnp.where(in_last, 0.0, pltpu.roll(at(slot, c), lanes - nv, 1))

        for slot in range(TAIL + 1 if strips else AFTER + 1):
            v = [at(slot, c) for c in range(comps)]
            weight = [coef[slot, kind, first_row, :] for kind in range(kinds)]
            total = weight[comps] * (v[0] + v[1] + v[2])
            for c in range(comps):
                if masked:
                    sides = shifted(slot, c)
                else:
                    sides = src[slot, c, rows(-1), :] + src[slot, c, rows(1), :]
                beside = sides + (up_of(slot, c) + down_of(slot, c))
                inside = row_in.get(slot)
                if masked:
                    beside = beside * (col_in if inside is None else col_in * inside)
                elif inside is not None:
                    beside = beside * inside
                emit(slot, c, weight[c] * v[c] + total - beside)

    def apply(src, strips, emit_rows, emit_margin):
        def body(j, carry):
            base = 16 * j

            def rows(d):
                start = 8 + base + d
                return pl.ds(pl.multiple_of(start, 8) if d == 0 else start, 16)

            def emit(slot, c, value):
                emit_rows(slot, c, pl.multiple_of(base, 16), value)

            operator(src, rows, pl.ds(pl.multiple_of(base, 16), 16), 16, None, strips, emit)
            return carry

        lax.fori_loop(0, cy // 16, body, 0)

        def shifted(slot, c):
            left = jnp.where(octet_row == H, 0.0, src[slot, c, 7 + cy : 15 + cy, :])
            return left + jnp.where(octet_row == H - 1, 0.0, src[slot, c, 1:9, :])

        operator(src, lambda d: top, slice(cy, cy + 8), 8, shifted, strips, emit_margin)

    def store(dst, split_too=False):
        def emit_rows(slot, c, base, value):
            dst[slot, c, pl.ds(base + 8, 16), :] = value
            if split_too and slot < HEAD:
                high2[slot, c, pl.ds(base, 16), :], low2[slot, c, pl.ds(base, 16), :] = split(value)

        def emit_margin(slot, c, value):
            dst[slot, c, low, :] = value
            dst[slot, c, top, :] = value

        return emit_rows, emit_margin

    apply(v0, True, *store(x1))
    apply(x1, True, *store(x2, True))

    def split_rows(slot, c, base, value):
        high3[slot, c, pl.ds(base, 16), :], low3[slot, c, pl.ds(base, 16), :] = split(value)

    def keep_margin(slot, c, value):
        margin3[slot, c] = value

    def fold(z):
        return sum(pltpu.roll(z[b * nv : (b + 1) * nv], (z.shape[1] - b * nv) % z.shape[1], 1) if b else z[:nv] for b in range(H))

    def flat(ref, first, count):
        return ref[first : first + count].reshape(count * comps * cy, lanes)

    chunks = range(0, AFTER + 1, 2)
    octet_margins = [x2[slot, c, top, :] for slot in range(AFTER + 1) for c in range(comps)]
    margin_h2, margin_l2 = split(jnp.concatenate(octet_margins, axis=0))

    def gram_m():
        def part(h2, l2):
            return dot(h2, jnp.concatenate([h2, l2], axis=1), TN)
        main = part(margin_h2, margin_l2)
        for first in chunks:
            main = main + part(flat(high2, first, 2), flat(low2, first, 2))
        main = fold(main)
        mixed = main[:, lanes : lanes + nv]
        return main[:, :nv] + (mixed + mixed.T)

    def gram_n():
        def part(h2, l2, h3, l3):
            return dot(h2, jnp.concatenate([h3, l3], axis=1), TN), dot(l2, h3, TN)
        h3, l3 = split(margin3[...].reshape((AFTER + 1) * comps * 8, lanes))
        main, cross = part(margin_h2, margin_l2, h3, l3)
        for first in chunks:
            more = part(*(flat(ref, first, 2) for ref in (high2, low2, high3, low3)))
            main, cross = main + more[0], cross + more[1]
        main = fold(main)
        return main[:, :nv] + main[:, lanes : lanes + nv] + fold(cross)[:, :nv]

    gram = gram_m()
    apply(x2, False, split_rows, keep_margin)
    pad = jnp.zeros((nv, lanes - nv), F32)
    inverse = inverse_factor(jnp.concatenate([gram, pad], axis=1), nv)[:, :nv]
    inverse = jnp.where(iota((nv, nv), 0) < rank_ref[0, 0], inverse, 0.0)
    image = gram_n()

    def rim(strip, first, block, own_first):
        own, other = [], []
        for at, weight_at in ((mid, slice(0, cy)), (top, slice(cy, cy + 8))):
            for c in range(comps):
                held = [x2[first + i, c, at, block * nv : (block + 1) * nv] for i in range(H)]
                weight = coef[strip, c, weight_at, :] + coef[strip, comps, weight_at, :]
                own.append(jnp.concatenate(held, axis=1) * weight)
                other.append(x2[strip, c, at, :])
        own.append(jnp.zeros((8, lanes), F32))
        other.append(jnp.zeros((8, lanes), F32))
        own, other = jnp.concatenate(own, axis=0), jnp.concatenate(other, axis=0)
        a, b = (own, other) if own_first else (other, own)
        return fold(dot3(a, b, TN))[:, :nv]

    rim_next = rim(TAIL, OWN - H, H - 1, True) * has_after
    rim_prev = rim(HEAD, 0, 0, True) * has_before

    start = start_ref[...]
    k2 = start.shape[0]
    products = dot3(jnp.concatenate([inverse.T, start], axis=0), inverse, NN)
    pack_ref[0, :nv] = jnp.concatenate([rim_prev, 0.5 * image, rim_next, products[:nv]], axis=1)
    starts = [products[nv + i : nv + i + 8] for i in range(0, k2, 8)]
    pad = jnp.zeros((8, lanes - nv * len(starts)), F32)
    pack_ref[0, nv:] = jnp.concatenate(starts + [pad], axis=1)


def prolong(coefs, high_ref, low_ref, out_ref, buf, sems):
    k2, nv = coefs.shape
    comps, cx = buf.shape[0], buf.shape[2]
    cy = buf.shape[3]
    own = cx // H
    tiled = jnp.concatenate([coefs] * H, axis=1)
    tiled = jnp.broadcast_to(tiled[:, None, :], (k2, 8, H * nv)).reshape(8 * k2, H * nv)
    same = lax.rem(iota(tiled.shape, 0), 8) == iota(tiled.shape, 1) // nv
    high, low = split(jnp.where(same, tiled, 0.0))
    left = jnp.concatenate([high, low, high], axis=1)
    copies = []
    for c in range(comps):
        for p in range(own):
            bh, bl = high_ref[p, c], low_ref[p, c]
            out = dot(left, jnp.concatenate([bh, bh, bl], axis=1), NT).reshape(k2, 8, cy)
            buf[c, :, pl.ds(p, H, stride=own), :] = out[:, :H]
        copies.append(pltpu.make_async_copy(buf.at[c], out_ref.at[:, c], sems.at[c]))
        copies[-1].start()
    for copy in copies:
        copy.wait()


def level_kernel(spans, order, factor, *refs):
    parts, (high_ref, low_ref, out_ref, packs, buf, sems) = refs[:-6], refs[-6:]
    k2 = buf.shape[1]
    nv = packs.shape[1] - 8
    n = spans * nv
    s = lax.axis_index("sub")
    index = 0
    for part in parts:
        for i in range(part.shape[0]):
            packs[order[index]] = part[i]
            index += 1
    lane = iota((nv, 128), 1)

    def placed(block, offset, first, last):
        rolled = pltpu.roll(block, offset % 128, 1) if offset % 128 else block
        at = iota(block.shape, 1) - offset
        tiles = [jnp.where((at + m >= first) & (at + m < last), rolled, 0.0) for m in range(0, n, 128)]
        return jnp.concatenate(tiles, axis=1)

    rows, products = [], []
    u = jnp.zeros((k2, n), F32)
    for b in range(spans):
        pack = packs[jnp.bitwise_xor(s, b)]
        rows.append(placed(pack[:nv], nv * (b - 1), 0, 3 * nv))
        products.append(placed(pack[:nv], nv * (b - 3), 3 * nv, 4 * nv))
        starts = [placed(pack[nv:], nv * (b - i), nv * i, nv * i + nv) for i in range(k2 // 8)]
        u = u + jnp.concatenate(starts, axis=0)
    rows = jnp.concatenate(rows, axis=0)
    full = split(rows + rows.T)
    products = split(jnp.concatenate(products, axis=0))

    def times(x, halves):
        xh, xl = split(x)
        out = dot(jnp.concatenate([xh, xl], axis=0), halves[0], NN)
        return out[:k2] + (out[k2:] + dot(xh, halves[1], NN))

    z = times(times(times(u, full), products), full)
    w = times(z, products)
    gram = dot3(w, z, NT)
    gram = jnp.concatenate([gram, jnp.zeros((k2, 128 - k2), F32)], axis=1)
    own = pltpu.roll(w, lax.rem(n - nv * s, n), 1)[:, :nv]
    coefs = dot3(inverse_factor(gram, k2)[:, :k2], factor * own, NN)
    prolong(coefs, high_ref, low_ref, out_ref, buf, sems)


def pairs(count, offset):
    return [q for i in range(offset, count - 1, 2) for q in ((i, i + 1), (i + 1, i))]


def from_behind(block, axis, distance):
    devices = range(lax.axis_size(axis))
    return lax.ppermute(block, axis, [(i - distance, i) for i in devices if i - distance in devices])


def level_coefs(pack, nv, k2, factor):
    highest = lax.Precision.HIGHEST
    rim_prev, half, rim_next, product = (pack[:nv, nv * i : nv * i + nv] for i in range(4))
    u = jnp.concatenate([pack[nv:, nv * i : nv * i + nv] for i in range(k2 // 8)], axis=0).T
    own = half + half.T
    rim = rim_next + from_behind(rim_prev, "sub", -1).T
    rim_before = from_behind(rim, "sub", 1)
    for step in range(2):
        z = jnp.dot(own, u, precision=highest)
        z = z + jnp.dot(rim, from_behind(u, "sub", -1), precision=highest)
        z = z + jnp.dot(rim_before.T, from_behind(u, "sub", 1), precision=highest)
        u = jnp.dot(product, z, precision=highest)
    lower = jnp.linalg.cholesky(lax.psum(jnp.dot(z.T, u, precision=highest), "sub"))
    return factor * lax.linalg.triangular_solve(lower, u.T, left_side=True, lower=True)


def in_vmem(x):
    return pltpu.with_memory_space_constraint(x, pltpu.VMEM)


def call(kernel, out_shape, scratch, name, in_specs=None, **more):
    return pl.pallas_call(
        kernel,
        out_shape=out_shape,
        scratch_shapes=scratch,
        compiler_params=pltpu.CompilerParams(vmem_limit_bytes=VMEM_MIB * MIB),
        name=name,
        **({"in_specs": in_specs} if in_specs else {}),
        **more,
    )


def on_device(start_vectors, stiffness, coupling, kept_ranks, level_start):
    spans, sects = lax.axis_size("sub"), lax.axis_size("sec")
    nv, comps, cx, cy = start_vectors.shape
    k2 = level_start.shape[1]
    channels = comps + 1
    slots = slots_of(cx)[-1] + 1
    shape = jax.ShapeDtypeStruct
    vmem = pl.BlockSpec(memory_space=pltpu.VMEM)
    hbm = pl.BlockSpec(memory_space=pltpu.HBM)

    pieces = (cx // H + 2) * comps + 1
    inputs = (start_vectors, stiffness, coupling, level_start.T)
    sec_shape = shape((-(-pieces // 2) * 8, cy), BF16)
    own, kt, sec_a, sec_b, start = call(
        pack_kernel,
        (shape((cx // H + 2, comps, cy, H * nv), BF16), shape((cy, channels * cx), BF16), sec_shape, sec_shape)
        + (shape((k2, nv), F32),),
        [
            pltpu.VMEM((comps, nv, cx, cy), BF16),
            pltpu.VMEM(stiffness.shape, BF16),
            pltpu.VMEM(coupling.shape, BF16),
            pltpu.VMEM((comps, nv * cx, cy), F32),
            pltpu.VMEM((channels * cx, cy), F32),
            pltpu.SemaphoreType.DMA((comps + 3,)),
        ],
        "pack",
        [hbm] * 4,
    )(*(pltpu.with_memory_space_constraint(x, pltpu.HBM) for x in inputs))
    sec_a = lax.ppermute(sec_a, "sec", pairs(sects, 0))
    sec_b = lax.ppermute(sec_b, "sec", pairs(sects, 1))
    sub_shape = shape((channels * (cy + 8), H * nv), BF16)
    sub_a, sub_b = call(edge_kernel, (sub_shape, sub_shape), [], "edge")(own, kt, sec_a, sec_b)
    sub_a = lax.ppermute(sub_a, "sub", pairs(spans, 0))
    sub_b = lax.ppermute(sub_b, "sub", pairs(spans, 1))

    def fine(*refs):
        fine_kernel((spans, sects), *refs)

    rows = shape((slots, comps, cy + 16, H * nv), F32)
    weights = shape((slots, channels, cy + 8, H * nv), F32)
    half = shape((slots - 2, comps, cy, H * nv), BF16)
    v0, coef = (in_vmem(x) for x in call(prep_kernel, (rows, weights), [], "prep")(own, kt))
    pack, high, low, _, _ = call(
        fine,
        (shape((1, nv + 8, cy), F32), half, half, rows, weights),
        [
            pltpu.VMEM(rows.shape, F32),
            pltpu.VMEM(rows.shape, F32),
            pltpu.VMEM(half.shape, BF16),
            pltpu.VMEM(half.shape, BF16),
            pltpu.VMEM((slots - 2, comps, 8, H * nv), F32),
        ],
        "fine",
        [pl.BlockSpec(memory_space=pltpu.SMEM)] + [vmem] * 8,
        input_output_aliases={2: 3, 3: 4},
    )(kept_ranks, start, v0, coef, kt, sec_a, sec_b, sub_a, sub_b)

    factor = math.sqrt(spans * comps * (cx + 2 * H) * (cy + 2 * H))
    result = shape((k2, comps, cx, cy), F32)
    tiles = [pltpu.VMEM((comps, k2, cx, cy), F32), pltpu.SemaphoreType.DMA((comps,))]
    if spans != 8:

        def prolong_kernel(coefs_ref, *refs):
            prolong(coefs_ref[...], *refs)

        coefs = level_coefs(pack[0], nv, k2, factor)
        return call(prolong_kernel, result, tiles, "prolong", [vmem] * 3, out_specs=hbm)(coefs, high, low)

    def swapped(block, bit):
        return lax.ppermute(block, "sub", [(i, i ^ bit) for i in range(spans)])

    far = swapped(pack, 4)
    both = jnp.concatenate([pack, far])
    parts = [both] + [swapped(both, bit) for bit in (2, 1, 3)]
    order = [high_bit ^ bit for bit in (0, 2, 1, 3) for high_bit in (0, 4)]

    def level(*refs):
        level_kernel(spans, order, factor, *refs)

    packs = pltpu.VMEM((spans,) + pack.shape[1:], F32)
    return call(level, result, [packs] + tiles, "level", [vmem] * 6, out_specs=hbm)(*parts, high, low)


def solution(mesh):
    placed = (
        P(None, None, "sub", "sec"),
        P(None, "sub", "sec"),
        P("sub", "sec"),
        P("sub", "sec"),
        P("sub", None),
    )
    return jax.shard_map(
        on_device,
        mesh=mesh,
        in_specs=placed,
        out_specs=P(None, None, "sub", "sec"),
        check_vma=False,
    )
```

```python
import math

import jax
import jax.numpy as jnp
from jax import lax
from jax.experimental import pallas as pl
from jax.experimental.pallas import tpu as pltpu
from jax.sharding import PartitionSpec as P

H = 4
MIB = 1 << 20
VMEM_MIB = 24
F32 = jnp.float32
BF16 = jnp.bfloat16
NN = (((1,), (0,)), ((), ()))
NT = (((1,), (1,)), ((), ()))
TN = (((0,), (0,)), ((), ()))


def iota(shape, dim):
    return lax.broadcasted_iota(jnp.int32, shape, dim)


def split(x):
    high = x.astype(BF16)
    return high, (x - high.astype(F32)).astype(BF16)


def dot(a, b, dims):
    return lax.dot_general(a, b, dims, preferred_element_type=F32)


def dot3(a, b, dims):
    (ah, al), (bh, bl) = split(a), split(b)
    return dot(ah, bh, dims) + (dot(ah, bl, dims) + dot(al, bh, dims))


def inverse_factor(gram, size, step=16):
    row, lane = iota((size, 128), 0), iota((size, 128), 1)
    work = jnp.where(lane < size, gram, jnp.where(lane == row + size, 1.0, 0.0))
    for first in range(0, size, step):
        columns = [jnp.broadcast_to(work[:, j : j + 1], (size, 128)) for j in range(first, first + step)]
        update = None
        for i, j in enumerate(range(first, min(first + step, size - 1))):
            factor = jnp.where(row > j, columns[i] / columns[i][j : j + 1, :], 0.0)
            for later in range(i + 1, step):
                columns[later] = columns[later] - factor * columns[later][j : j + 1, :]
            pivot = work[j : j + 1, :]
            if update is not None:
                pivot = pivot - update[j : j + 1, :]
            update = factor * pivot if update is None else update + factor * pivot
        work = work - update
    diag = jnp.sum(jnp.where(lane == row, work, 0.0), axis=1, keepdims=True)
    return pltpu.roll(work / jnp.sqrt(diag), 128 - size, 1)


def slots_of(cx):
    own = cx // H
    return own, own, own + 1, own + 2, own + 3


def halves(octet_a, octet_b):
    return jnp.where(iota(octet_a.shape, 0) < H, octet_a, octet_b)


def swap(octet):
    return pltpu.roll(octet, H, 0)


def pack_kernel(
    v_hbm, k_hbm, g_hbm, start_hbm, own_ref, kt_ref, sec_a, sec_b, start_ref, v_buf, k_buf, g_buf, vf, kf, sems
):
    comps, nv, cx, cy = v_buf.shape
    copies = [pltpu.make_async_copy(v_hbm.at[:, c], v_buf.at[c], sems.at[c]) for c in range(comps)]
    copies.append(pltpu.make_async_copy(k_hbm, k_buf, sems.at[comps]))
    copies.append(pltpu.make_async_copy(g_hbm, g_buf, sems.at[comps + 1]))
    copies.append(pltpu.make_async_copy(start_hbm, start_ref, sems.at[comps + 2]))
    for copy in copies:
        copy.start()
    sec_even = lax.rem(lax.axis_index("sec"), 2) == 0
    own = cx // H
    pieces = (own + 2) * comps + 1
    firsts, lasts = [None] * pieces, [None] * pieces
    for c in range(comps):
        copies[c].wait()
        for a in range(nv):
            vf[c, (cx + 8) * a : (cx + 8) * a + cx] = v_buf[c, a].astype(F32)
        for p in range(own + 2):
            rows = [b * own + p for b in range(H)] if p < own else [b + (p - own) * (cx - H) for b in range(H)]
            stack = [vf[c, pl.ds(x, nv, stride=cx + 8), :] for x in rows]
            turned = jnp.concatenate(stack, axis=0).astype(BF16).T
            own_ref[p, c] = turned
            firsts[p * comps + c] = turned[:16].astype(F32)[:8]
            lasts[p * comps + c] = turned[cy - 16 :].astype(F32)[8:]
    for copy in copies[comps:]:
        copy.wait()
    kf[: comps * cx] = k_buf[...].astype(F32).reshape(comps * cx, cy)
    kf[comps * cx :] = g_buf[...].astype(F32)
    turned = kf[...].T
    kt_ref[...] = turned.astype(BF16)
    firsts[-1], lasts[-1] = turned[:8], turned[cy - 8 :]
    for octets in (firsts, lasts):
        if len(octets) % 2:
            octets.append(jnp.zeros((8, cy), F32))
    pairs_of = range(0, len(firsts), 2)
    left = [halves(firsts[q], swap(firsts[q + 1])) for q in pairs_of]
    right = [halves(swap(lasts[q]), lasts[q + 1]) for q in pairs_of]
    left, right = jnp.concatenate(left, axis=0), jnp.concatenate(right, axis=0)
    sec_a[...] = jnp.where(sec_even, right, left).astype(BF16)
    sec_b[...] = jnp.where(sec_even, left, right).astype(BF16)


def margin_octets(sec_a, sec_b, sec_even, count):
    a, b = sec_a[...].astype(F32), sec_b[...].astype(F32)
    hi, lo = jnp.where(sec_even, a, b), jnp.where(sec_even, b, a)
    out = []
    for q in range(count):
        at = slice(8 * (q // 2), 8 * (q // 2) + 8)
        out.append(halves(swap(hi[at]), lo[at]) if q % 2 else halves(hi[at], swap(lo[at])))
    return out


def edge_kernel(own_ref, kt_ref, sec_a, sec_b, sub_a, sub_b):
    slots, comps, cy, lanes = own_ref.shape
    sub_even = lax.rem(lax.axis_index("sub"), 2) == 0
    sec_even = lax.rem(lax.axis_index("sec"), 2) == 0
    octets = margin_octets(sec_a, sec_b, sec_even, slots * comps + 1)
    first, last = slots - 2, slots - 1
    head = octets[first * comps : first * comps + comps] + octets[-1:]
    tail = octets[last * comps : last * comps + comps] + octets[-1:]
    head, tail = jnp.concatenate(head, axis=0), jnp.concatenate(tail, axis=0)
    for ref, to_next in ((sub_a, sub_even), (sub_b, jnp.logical_not(sub_even))):
        slot = jnp.where(to_next, last, first)
        for c in range(comps):
            ref[c * cy : (c + 1) * cy] = own_ref[slot, c]
        ref[comps * cy : (comps + 1) * cy] = kt_ref[...]
        ref[(comps + 1) * cy :] = jnp.where(to_next, tail, head).astype(BF16)


def spread(table, wanted, kinds, cx):
    lanes = table.shape[1]
    source = iota((lanes, lanes), 0)
    pick = [jnp.where(source == kind * cx + wanted, 1.0, 0.0).astype(BF16) for kind in range(kinds)]
    out = dot(table, jnp.concatenate(pick, axis=1), NN)
    return [out[:, kind * lanes : (kind + 1) * lanes] for kind in range(kinds)]


def terms_of(rows):
    return [4.0 + k - rows[-1] for k in rows[:-1]] + [rows[-1]]


def row_of_slot(p, own, cx, block):
    return block * own + p if p < own else block + (p - own) * (cx - H)


def prep_kernel(own_ref, kt_ref, v0, coef):
    slots, comps, cy, lanes = own_ref.shape
    own, kinds = slots - 2, comps + 1
    cx = kt_ref.shape[1] // kinds
    head = slots_of(cx)[3]
    block = iota((lanes, lanes), 1) // (lanes // H)
    for p in range(slots):
        slot = p if p < own else head + p - own
        for c in range(comps):
            v0[slot, c, 8 : 8 + cy, :] = own_ref[p, c].astype(F32)
        values = spread(kt_ref[...], row_of_slot(p, own, cx, block), kinds, cx)
        for kind, value in enumerate(terms_of(values)):
            coef[slot, kind, :cy, :] = value


def fine_kernel(sizes, rank_ref, start_ref, v0_in, coef_in, kt_ref, sec_a, sec_b, sub_a, sub_b, pack_ref, high2, low2, v0, coef, x1, x2, high3, low3, margin3):
    spans, sects = sizes
    _, comps, cy, lanes = high2.shape
    nv = start_ref.shape[1]
    cx = kt_ref.shape[1] // (comps + 1)
    OWN, BEFORE, AFTER, HEAD, TAIL = slots_of(cx)
    s, t = lax.axis_index("sub"), lax.axis_index("sec")
    sub_even, sec_even = lax.rem(s, 2) == 0, lax.rem(t, 2) == 0
    kinds = comps + 1
    low, top = slice(0, 8), slice(8 + cy, 16 + cy)
    mid = slice(8, 8 + cy)
    octets = margin_octets(sec_a, sec_b, sec_even, (OWN + 2) * comps + 1)

    def put_octet(slot, c, octet):
        v0[slot, c, low, :] = octet
        v0[slot, c, top, :] = octet

    def received(first, count):
        a, b = sub_a[first : first + count].astype(F32), sub_b[first : first + count].astype(F32)
        return jnp.where(sub_even, a, b), jnp.where(sub_even, b, a)

    for c in range(comps):
        for p in range(OWN + 2):
            put_octet(p if p < OWN else HEAD + p - OWN, c, octets[p * comps + c])
        v0[AFTER, c, mid, :], v0[BEFORE, c, mid, :] = received(c * cy, cy)
        after_octet, before_octet = received(kinds * cy + 8 * c, 8)
        put_octet(BEFORE, c, before_octet)
        put_octet(AFTER, c, after_octet)

    octet_row = iota((8, lanes), 0)
    col_in = jnp.where(octet_row < H, jnp.where(t < sects - 1, 1.0, 0.0), jnp.where(t > 0, 1.0, 0.0))
    has_before, has_after = jnp.where(s > 0, 1.0, 0.0), jnp.where(s < spans - 1, 1.0, 0.0)
    row_in = {BEFORE: has_before, AFTER: has_after}
    octet_block = iota((8, lanes), 1) // nv
    for p in range(OWN + 2):
        slot = p if p < OWN else HEAD + p - OWN
        wanted = row_of_slot(p, OWN, cx, octet_block)
        rows = [jnp.take_along_axis(octets[-1], wanted + kind * cx, axis=1) for kind in range(kinds)]
        for kind, value in enumerate(terms_of(rows)):
            coef[slot, kind, cy : cy + 8, :] = value * col_in
    after, before = received(comps * cy, cy)
    after_octet, before_octet = received(kinds * cy + 8 * comps, 8)
    block = iota((lanes, lanes), 1) // nv
    for slot, rows, octet, p in ((AFTER, after, after_octet, OWN), (BEFORE, before, before_octet, OWN + 1)):
        table = jnp.concatenate([rows, octet, jnp.zeros_like(octet)], axis=0).astype(BF16)
        values = spread(table, row_of_slot(p, OWN, cx, block), kinds, cx)
        for kind, value in enumerate(terms_of(values)):
            coef[slot, kind, :cy, :] = value[:cy] * row_in[slot]
            coef[slot, kind, cy : cy + 8, :] = value[cy : cy + 8] * (col_in * row_in[slot])

    def operator(src, rows, first_row, length, shifted, strips, emit):
        lane = iota((length, lanes), 1)
        in_first, in_last = lane < nv, lane >= lanes - nv
        masked = shifted is not None

        def at(slot, c):
            return src[slot, c, rows(0), :]

        def up_of(slot, c):
            if 0 < slot < OWN:
                return at(slot - 1, c)
            if slot in (0, AFTER):
                return pltpu.roll(jnp.where(in_last, at(BEFORE if slot == 0 else OWN - 1, c), at(OWN - 1 if slot == 0 else AFTER, c)), nv, 1)
            if slot == HEAD:
                return pltpu.roll(jnp.where(in_last, at(BEFORE, c), at(HEAD, c)), nv, 1)
            return jnp.where(in_first, 0.0, pltpu.roll(at(slot, c), nv, 1))

        def down_of(slot, c):
            if slot < OWN - 1:
                return at(slot + 1, c)
            if slot in (OWN - 1, BEFORE):
                return pltpu.roll(jnp.where(in_first, at(AFTER if slot == OWN - 1 else 0, c), at(0 if slot == OWN - 1 else BEFORE, c)), lanes - nv, 1)
            if slot == TAIL:
                return pltpu.roll(jnp.where(in_first, at(AFTER, c), at(TAIL, c)), lanes - nv, 1)
            return jnp.where(in_last, 0.0, pltpu.roll(at(slot, c), lanes - nv, 1))

        for slot in range(TAIL + 1 if strips else AFTER + 1):
            v = [at(slot, c) for c in range(comps)]
            weight = [coef[slot, kind, first_row, :] for kind in range(kinds)]
            total = weight[comps] * (v[0] + v[1] + v[2])
            for c in range(comps):
                if masked:
                    sides = shifted(slot, c)
                else:
                    sides = src[slot, c, rows(-1), :] + src[slot, c, rows(1), :]
                beside = sides + (up_of(slot, c) + down_of(slot, c))
                inside = row_in.get(slot)
                if masked:
                    beside = beside * (col_in if inside is None else col_in * inside)
                elif inside is not None:
                    beside = beside * inside
                emit(slot, c, weight[c] * v[c] + total - beside)

    def apply(src, strips, emit_rows, emit_margin):
        def body(j, carry):
            base = 16 * j

            def rows(d):
                start = 8 + base + d
                return pl.ds(pl.multiple_of(start, 8) if d == 0 else start, 16)

            def emit(slot, c, value):
                emit_rows(slot, c, pl.multiple_of(base, 16), value)

            operator(src, rows, pl.ds(pl.multiple_of(base, 16), 16), 16, None, strips, emit)
            return carry

        lax.fori_loop(0, cy // 16, body, 0, unroll=True)

        def shifted(slot, c):
            left = jnp.where(octet_row == H, 0.0, src[slot, c, 7 + cy : 15 + cy, :])
            return left + jnp.where(octet_row == H - 1, 0.0, src[slot, c, 1:9, :])

        operator(src, lambda d: top, slice(cy, cy + 8), 8, shifted, strips, emit_margin)

    def store(dst, split_too=False):
        def emit_rows(slot, c, base, value):
            dst[slot, c, pl.ds(base + 8, 16), :] = value
            if split_too and slot < HEAD:
                high2[slot, c, pl.ds(base, 16), :], low2[slot, c, pl.ds(base, 16), :] = split(value)

        def emit_margin(slot, c, value):
            dst[slot, c, low, :] = value
            dst[slot, c, top, :] = value

        return emit_rows, emit_margin

    apply(v0, True, *store(x1))
    apply(x1, True, *store(x2, True))

    def split_rows(slot, c, base, value):
        high3[slot, c, pl.ds(base, 16), :], low3[slot, c, pl.ds(base, 16), :] = split(value)

    def keep_margin(slot, c, value):
        margin3[slot, c] = value

    def fold(z):
        return sum(pltpu.roll(z[b * nv : (b + 1) * nv], (z.shape[1] - b * nv) % z.shape[1], 1) if b else z[:nv] for b in range(H))

    def flat(ref, first, count):
        return ref[first : first + count].reshape(count * comps * cy, lanes)

    chunks = range(0, AFTER + 1, 2)
    octet_margins = [x2[slot, c, top, :] for slot in range(AFTER + 1) for c in range(comps)]
    margin_h2, margin_l2 = split(jnp.concatenate(octet_margins, axis=0))

    def gram_m():
        def part(h2, l2):
            return dot(h2, jnp.concatenate([h2, l2], axis=1), TN)
        main = part(margin_h2, margin_l2)
        for first in chunks:
            main = main + part(flat(high2, first, 2), flat(low2, first, 2))
        main = fold(main)
        mixed = main[:, lanes : lanes + nv]
        return main[:, :nv] + (mixed + mixed.T)

    def gram_n():
        def part(h2, l2, h3, l3):
            return dot(h2, jnp.concatenate([h3, l3], axis=1), TN), dot(l2, h3, TN)
        h3, l3 = split(margin3[...].reshape((AFTER + 1) * comps * 8, lanes))
        main, cross = part(margin_h2, margin_l2, h3, l3)
        for first in chunks:
            more = part(*(flat(ref, first, 2) for ref in (high2, low2, high3, low3)))
            main, cross = main + more[0], cross + more[1]
        main = fold(main)
        return main[:, :nv] + main[:, lanes : lanes + nv] + fold(cross)[:, :nv]

    gram = gram_m()
    apply(x2, False, split_rows, keep_margin)
    pad = jnp.zeros((nv, lanes - nv), F32)
    inverse = inverse_factor(jnp.concatenate([gram, pad], axis=1), nv)[:, :nv]
    inverse = jnp.where(iota((nv, nv), 0) < rank_ref[0, 0], inverse, 0.0)
    image = gram_n()

    def rim(strip, first, block):
        def rows_of(slot, weighted):
            out = []
            for at, weight_at in ((mid, slice(0, cy)), (top, slice(cy, cy + 8))):
                for c in range(comps):
                    rows = x2[slot, c, at, :]
                    if weighted:
                        rows = rows * (coef[slot, c, weight_at, :] + coef[slot, comps, weight_at, :])
                    out.append(rows)
            return out

        pad = [jnp.zeros((8, lanes), F32)]
        turned = [half.T for half in split(jnp.concatenate(rows_of(strip, True) + pad, axis=0))]
        total = jnp.zeros((2 * nv, 2 * lanes), F32)
        for i in range(H):
            margin = split(jnp.concatenate([x2[first + i, c, top, :] for c in range(comps)] + pad, axis=0))
            own = [
                jnp.concatenate([ref[first + i, c] for c in range(comps)] + [rest], axis=0)
                for ref, rest in zip((high2, low2), margin)
            ]
            other = jnp.concatenate([half[i * nv : (i + 1) * nv] for half in turned], axis=0)
            total = total + dot(other, jnp.concatenate(own, axis=1), NN)
        total = total[:nv] + total[nv:]
        total = total[:, :lanes] + total[:, lanes:]
        return total[:, block * nv : (block + 1) * nv].T

    rim_next = rim(TAIL, OWN - H, H - 1) * has_after
    rim_prev = rim(HEAD, 0, 0) * has_before

    start = start_ref[...]
    k2 = start.shape[0]
    products = dot3(jnp.concatenate([inverse.T, start], axis=0), inverse, NN)
    pack_ref[0, :nv] = jnp.concatenate([rim_prev, 0.5 * image, rim_next, products[:nv]], axis=1)
    starts = [products[nv + i : nv + i + 8] for i in range(0, k2, 8)]
    pad = jnp.zeros((8, lanes - nv * len(starts)), F32)
    pack_ref[0, nv:] = jnp.concatenate(starts + [pad], axis=1)


def prolong(coefs, high_ref, low_ref, out_ref, buf, sems):
    k2, nv = coefs.shape
    comps, cx = buf.shape[0], buf.shape[2]
    cy = buf.shape[3]
    own = cx // H
    tiled = jnp.concatenate([coefs] * H, axis=1)
    tiled = jnp.broadcast_to(tiled[:, None, :], (k2, 8, H * nv)).reshape(8 * k2, H * nv)
    same = lax.rem(iota(tiled.shape, 0), 8) == iota(tiled.shape, 1) // nv
    high, low = split(jnp.where(same, tiled, 0.0))
    left = jnp.concatenate([high, low, high], axis=1)
    copies = []
    for c in range(comps):
        for p in range(own):
            bh, bl = high_ref[p, c], low_ref[p, c]
            out = dot(left, jnp.concatenate([bh, bh, bl], axis=1), NT).reshape(k2, 8, cy)
            buf[c, :, pl.ds(p, H, stride=own), :] = out[:, :H]
        copies.append(pltpu.make_async_copy(buf.at[c], out_ref.at[:, c], sems.at[c]))
        copies[-1].start()
    for copy in copies:
        copy.wait()


def level_kernel(spans, order, factor, *refs):
    parts, (high_ref, low_ref, out_ref, packs, buf, sems) = refs[:-6], refs[-6:]
    k2 = buf.shape[1]
    nv = packs.shape[1] - 8
    n = spans * nv
    s = lax.axis_index("sub")
    index = 0
    for part in parts:
        for i in range(part.shape[0]):
            packs[order[index]] = part[i]
            index += 1
    lane = iota((nv, 128), 1)

    def placed(block, offset, first, last):
        rolled = pltpu.roll(block, offset % 128, 1) if offset % 128 else block
        at = iota(block.shape, 1) - offset
        tiles = [jnp.where((at + m >= first) & (at + m < last), rolled, 0.0) for m in range(0, n, 128)]
        return jnp.concatenate(tiles, axis=1)

    rows, products = [], []
    u = jnp.zeros((k2, n), F32)
    for b in range(spans):
        pack = packs[jnp.bitwise_xor(s, b)]
        rows.append(placed(pack[:nv], nv * (b - 1), 0, 3 * nv))
        products.append(placed(pack[:nv], nv * (b - 3), 3 * nv, 4 * nv))
        starts = [placed(pack[nv:], nv * (b - i), nv * i, nv * i + nv) for i in range(k2 // 8)]
        u = u + jnp.concatenate(starts, axis=0)
    rows = jnp.concatenate(rows, axis=0)
    full = split(rows + rows.T)
    products = split(jnp.concatenate(products, axis=0))

    def times(x, halves):
        xh, xl = split(x)
        out = dot(jnp.concatenate([xh, xl], axis=0), halves[0], NN)
        return out[:k2] + (out[k2:] + dot(xh, halves[1], NN))

    z = times(times(times(u, full), products), full)
    w = times(z, products)
    gram = dot3(w, z, NT)
    gram = jnp.concatenate([gram, jnp.zeros((k2, 128 - k2), F32)], axis=1)
    own = pltpu.roll(w, lax.rem(n - nv * s, n), 1)[:, :nv]
    coefs = dot3(inverse_factor(gram, k2)[:, :k2], factor * own, NN)
    prolong(coefs, high_ref, low_ref, out_ref, buf, sems)


def pairs(count, offset):
    return [q for i in range(offset, count - 1, 2) for q in ((i, i + 1), (i + 1, i))]


def from_behind(block, axis, distance):
    devices = range(lax.axis_size(axis))
    return lax.ppermute(block, axis, [(i - distance, i) for i in devices if i - distance in devices])


def level_coefs(pack, nv, k2, factor):
    highest = lax.Precision.HIGHEST
    rim_prev, half, rim_next, product = (pack[:nv, nv * i : nv * i + nv] for i in range(4))
    u = jnp.concatenate([pack[nv:, nv * i : nv * i + nv] for i in range(k2 // 8)], axis=0).T
    own = half + half.T
    rim = rim_next + from_behind(rim_prev, "sub", -1).T
    rim_before = from_behind(rim, "sub", 1)
    for step in range(2):
        z = jnp.dot(own, u, precision=highest)
        z = z + jnp.dot(rim, from_behind(u, "sub", -1), precision=highest)
        z = z + jnp.dot(rim_before.T, from_behind(u, "sub", 1), precision=highest)
        u = jnp.dot(product, z, precision=highest)
    lower = jnp.linalg.cholesky(lax.psum(jnp.dot(z.T, u, precision=highest), "sub"))
    return factor * lax.linalg.triangular_solve(lower, u.T, left_side=True, lower=True)


def in_vmem(x):
    return pltpu.with_memory_space_constraint(x, pltpu.VMEM)


def call(kernel, out_shape, scratch, name, in_specs=None, **more):
    return pl.pallas_call(
        kernel,
        out_shape=out_shape,
        scratch_shapes=scratch,
        compiler_params=pltpu.CompilerParams(vmem_limit_bytes=VMEM_MIB * MIB),
        name=name,
        **({"in_specs": in_specs} if in_specs else {}),
        **more,
    )


def on_device(start_vectors, stiffness, coupling, kept_ranks, level_start):
    spans, sects = lax.axis_size("sub"), lax.axis_size("sec")
    nv, comps, cx, cy = start_vectors.shape
    k2 = level_start.shape[1]
    channels = comps + 1
    slots = slots_of(cx)[-1] + 1
    shape = jax.ShapeDtypeStruct
    vmem = pl.BlockSpec(memory_space=pltpu.VMEM)
    hbm = pl.BlockSpec(memory_space=pltpu.HBM)

    pieces = (cx // H + 2) * comps + 1
    inputs = (start_vectors, stiffness, coupling, level_start.T)
    sec_shape = shape((-(-pieces // 2) * 8, cy), BF16)
    own, kt, sec_a, sec_b, start = call(
        pack_kernel,
        (shape((cx // H + 2, comps, cy, H * nv), BF16), shape((cy, channels * cx), BF16), sec_shape, sec_shape)
        + (shape((k2, nv), F32),),
        [
            pltpu.VMEM((comps, nv, cx, cy), BF16),
            pltpu.VMEM(stiffness.shape, BF16),
            pltpu.VMEM(coupling.shape, BF16),
            pltpu.VMEM((comps, nv * (cx + 8), cy), F32),
            pltpu.VMEM((channels * cx, cy), F32),
            pltpu.SemaphoreType.DMA((comps + 3,)),
        ],
        "pack",
        [hbm] * 4,
    )(*(pltpu.with_memory_space_constraint(x, pltpu.HBM) for x in inputs))
    sec_a = lax.ppermute(sec_a, "sec", pairs(sects, 0))
    sec_b = lax.ppermute(sec_b, "sec", pairs(sects, 1))
    sub_shape = shape((channels * (cy + 8), H * nv), BF16)
    sub_a, sub_b = call(edge_kernel, (sub_shape, sub_shape), [], "edge")(own, kt, sec_a, sec_b)
    sub_a = lax.ppermute(sub_a, "sub", pairs(spans, 0))
    sub_b = lax.ppermute(sub_b, "sub", pairs(spans, 1))

    def fine(*refs):
        fine_kernel((spans, sects), *refs)

    rows = shape((slots, comps, cy + 16, H * nv), F32)
    weights = shape((slots, channels, cy + 8, H * nv), F32)
    half = shape((slots - 2, comps, cy, H * nv), BF16)
    v0, coef = (in_vmem(x) for x in call(prep_kernel, (rows, weights), [], "prep")(own, kt))
    pack, high, low, _, _ = call(
        fine,
        (shape((1, nv + 8, cy), F32), half, half, rows, weights),
        [
            pltpu.VMEM(rows.shape, F32),
            pltpu.VMEM(rows.shape, F32),
            pltpu.VMEM(half.shape, BF16),
            pltpu.VMEM(half.shape, BF16),
            pltpu.VMEM((slots - 2, comps, 8, H * nv), F32),
        ],
        "fine",
        [pl.BlockSpec(memory_space=pltpu.SMEM)] + [vmem] * 8,
        input_output_aliases={2: 3, 3: 4},
    )(kept_ranks, start, v0, coef, kt, sec_a, sec_b, sub_a, sub_b)

    factor = math.sqrt(spans * comps * (cx + 2 * H) * (cy + 2 * H))
    result = shape((k2, comps, cx, cy), F32)
    tiles = [pltpu.VMEM((comps, k2, cx, cy), F32), pltpu.SemaphoreType.DMA((comps,))]
    if spans != 8:

        def prolong_kernel(coefs_ref, *refs):
            prolong(coefs_ref[...], *refs)

        coefs = level_coefs(pack[0], nv, k2, factor)
        return call(prolong_kernel, result, tiles, "prolong", [vmem] * 3, out_specs=hbm)(coefs, high, low)

    def swapped(block, bit):
        return lax.ppermute(block, "sub", [(i, i ^ bit) for i in range(spans)])

    far = swapped(pack, 4)
    both = jnp.concatenate([pack, far])
    parts = [both] + [swapped(both, bit) for bit in (2, 1, 3)]
    order = [high_bit ^ bit for bit in (0, 2, 1, 3) for high_bit in (0, 4)]

    def level(*refs):
        level_kernel(spans, order, factor, *refs)

    packs = pltpu.VMEM((spans,) + pack.shape[1:], F32)
    return call(level, result, [packs] + tiles, "level", [vmem] * 6, out_specs=hbm)(*parts, high, low)


def solution(mesh):
    placed = (
        P(None, None, "sub", "sec"),
        P(None, "sub", "sec"),
        P("sub", "sec"),
        P("sub", "sec"),
        P("sub", None),
    )
    return jax.shard_map(
        on_device,
        mesh=mesh,
        in_specs=placed,
        out_specs=P(None, None, "sub", "sec"),
        check_vma=False,
    )
```

```python
import math

import jax
import jax.numpy as jnp
from jax import lax
from jax.experimental import pallas as pl
from jax.experimental.pallas import tpu as pltpu
from jax.sharding import PartitionSpec as P

H = 4
MIB = 1 << 20
VMEM_MIB = 24
F32 = jnp.float32
BF16 = jnp.bfloat16
NN = (((1,), (0,)), ((), ()))
NT = (((1,), (1,)), ((), ()))
TN = (((0,), (0,)), ((), ()))


def iota(shape, dim):
    return lax.broadcasted_iota(jnp.int32, shape, dim)


def split(x):
    high = x.astype(BF16)
    return high, (x - high.astype(F32)).astype(BF16)


def dot(a, b, dims):
    return lax.dot_general(a, b, dims, preferred_element_type=F32)


def dot3(a, b, dims):
    (ah, al), (bh, bl) = split(a), split(b)
    return dot(ah, bh, dims) + (dot(ah, bl, dims) + dot(al, bh, dims))


def inverse_factor(gram, size, step=16):
    row, lane = iota((size, 128), 0), iota((size, 128), 1)
    work = jnp.where(lane < size, gram, jnp.where(lane == row + size, 1.0, 0.0))
    for first in range(0, size, step):
        columns = [jnp.broadcast_to(work[:, j : j + 1], (size, 128)) for j in range(first, first + step)]
        update = None
        for i, j in enumerate(range(first, min(first + step, size - 1))):
            factor = jnp.where(row > j, columns[i] / columns[i][j : j + 1, :], 0.0)
            for later in range(i + 1, step):
                columns[later] = columns[later] - factor * columns[later][j : j + 1, :]
            pivot = work[j : j + 1, :]
            if update is not None:
                pivot = pivot - update[j : j + 1, :]
            update = factor * pivot if update is None else update + factor * pivot
        work = work - update
    diag = jnp.sum(jnp.where(lane == row, work, 0.0), axis=1, keepdims=True)
    return pltpu.roll(work / jnp.sqrt(diag), 128 - size, 1)


def slots_of(cx):
    own = cx // H
    return own, own, own + 1, own + 2, own + 3


def halves(octet_a, octet_b):
    return jnp.where(iota(octet_a.shape, 0) < H, octet_a, octet_b)


def swap(octet):
    return pltpu.roll(octet, H, 0)


def narrowed(table, kinds, cx):
    wide = 2 * H * kinds
    parts = table.shape[1] // wide if table.shape[0] > 8 else 1
    count = table.shape[0] // parts
    lane = iota((count, table.shape[1]), 1)
    inner = lax.rem(lane, wide)
    side, kind, i = inner // (H * kinds), lax.rem(inner // H, kinds), lax.rem(inner, H)
    source = kind * cx + i + side * (cx - H)
    out = jnp.zeros((count, table.shape[1]), F32)
    for part in range(parts):
        picked = jnp.take_along_axis(table[part * count : (part + 1) * count], source, axis=1)
        out = picked if parts == 1 else jnp.where(lane // wide == part, picked, out)
    return out


def pack_kernel(
    v_hbm, k_hbm, g_hbm, start_hbm, own_ref, kt_ref, sec_a, sec_b, start_ref, narrow_ref, v_buf, k_buf, g_buf, vf, kf, sems
):
    comps, nv, cx, cy = v_buf.shape
    copies = [pltpu.make_async_copy(v_hbm.at[:, c], v_buf.at[c], sems.at[c]) for c in range(comps)]
    copies.append(pltpu.make_async_copy(k_hbm, k_buf, sems.at[comps]))
    copies.append(pltpu.make_async_copy(g_hbm, g_buf, sems.at[comps + 1]))
    copies.append(pltpu.make_async_copy(start_hbm, start_ref, sems.at[comps + 2]))
    for copy in copies:
        copy.start()
    sec_even = lax.rem(lax.axis_index("sec"), 2) == 0
    own = cx // H
    pieces = (own + 2) * comps + 1
    firsts, lasts = [None] * pieces, [None] * pieces
    for c in range(comps):
        copies[c].wait()
        for a in range(nv):
            vf[c, (cx + 8) * a : (cx + 8) * a + cx] = v_buf[c, a].astype(F32)
        for p in range(own + 2):
            rows = [b * own + p for b in range(H)] if p < own else [b + (p - own) * (cx - H) for b in range(H)]
            stack = [vf[c, pl.ds(x, nv, stride=cx + 8), :] for x in rows]
            turned = jnp.concatenate(stack, axis=0).astype(BF16).T
            own_ref[p, c] = turned
            firsts[p * comps + c] = turned[:16].astype(F32)[:8]
            lasts[p * comps + c] = turned[cy - 16 :].astype(F32)[8:]
    for copy in copies[comps:]:
        copy.wait()
    kf[: comps * cx] = k_buf[...].astype(F32).reshape(comps * cx, cy)
    kf[comps * cx :] = g_buf[...].astype(F32)
    turned = kf[...].T
    kt_ref[...] = turned.astype(BF16)
    narrow_ref[...] = narrowed(turned, comps + 1, cx).astype(BF16)
    firsts[-1], lasts[-1] = turned[:8], turned[cy - 8 :]
    for octets in (firsts, lasts):
        if len(octets) % 2:
            octets.append(jnp.zeros((8, cy), F32))
    pairs_of = range(0, len(firsts), 2)
    left = [halves(firsts[q], swap(firsts[q + 1])) for q in pairs_of]
    right = [halves(swap(lasts[q]), lasts[q + 1]) for q in pairs_of]
    left, right = jnp.concatenate(left, axis=0), jnp.concatenate(right, axis=0)
    sec_a[...] = jnp.where(sec_even, right, left).astype(BF16)
    sec_b[...] = jnp.where(sec_even, left, right).astype(BF16)


def margin_octets(sec_a, sec_b, sec_even, count):
    a, b = sec_a[...].astype(F32), sec_b[...].astype(F32)
    hi, lo = jnp.where(sec_even, a, b), jnp.where(sec_even, b, a)
    out = []
    for q in range(count):
        at = slice(8 * (q // 2), 8 * (q // 2) + 8)
        out.append(halves(swap(hi[at]), lo[at]) if q % 2 else halves(hi[at], swap(lo[at])))
    return out


def edge_kernel(cx, own_ref, narrow_ref, sec_a, sec_b, sub_a, sub_b):
    slots, comps, cy, lanes = own_ref.shape
    sub_even = lax.rem(lax.axis_index("sub"), 2) == 0
    sec_even = lax.rem(lax.axis_index("sec"), 2) == 0
    octets = margin_octets(sec_a, sec_b, sec_even, slots * comps + 1)
    first, last = slots - 2, slots - 1
    table = [narrowed(octets[-1], comps + 1, cx)]
    head = octets[first * comps : first * comps + comps] + table
    tail = octets[last * comps : last * comps + comps] + table
    head, tail = jnp.concatenate(head, axis=0), jnp.concatenate(tail, axis=0)
    for ref, to_next in ((sub_a, sub_even), (sub_b, jnp.logical_not(sub_even))):
        slot = jnp.where(to_next, last, first)
        for c in range(comps):
            ref[c * cy : (c + 1) * cy] = own_ref[slot, c]
        narrow = comps * cy + narrow_ref.shape[0]
        ref[comps * cy : narrow] = narrow_ref[...]
        ref[narrow:] = jnp.where(to_next, tail, head).astype(BF16)


def spread(table, wanted, kinds, cx):
    lanes = table.shape[1]
    source = iota((lanes, lanes), 0)
    pick = [jnp.where(source == kind * cx + wanted, 1.0, 0.0).astype(BF16) for kind in range(kinds)]
    out = dot(table, jnp.concatenate(pick, axis=1), NN)
    return [out[:, kind * lanes : (kind + 1) * lanes] for kind in range(kinds)]


def terms_of(rows):
    return [4.0 + k - rows[-1] for k in rows[:-1]] + [rows[-1]]


def row_of_slot(p, own, cx, block):
    return block * own + p if p < own else block + (p - own) * (cx - H)


def operator(src, coef, nv, rows, weight_rows, sides_of, slots, margins, inside_of, emit):
    count, comps, _, lanes = src.shape
    OWN = count - 4
    BEFORE, AFTER, HEAD, TAIL = range(OWN, count)

    def at(slot, c):
        return src[slot, c, rows, :]

    lane = iota(at(0, 0).shape, 1)
    in_first, in_last = lane < nv, lane >= lanes - nv

    def up_of(slot, c):
        if 0 < slot < OWN:
            return at(slot - 1, c)
        last, margin = {0: (OWN - 1, BEFORE), AFTER: (AFTER, OWN - 1), HEAD: (HEAD, BEFORE)}.get(slot, (slot, None))
        if margin is None or (margin == BEFORE and not margins):
            return jnp.where(in_first, 0.0, pltpu.roll(at(last, c), nv, 1))
        return pltpu.roll(jnp.where(in_last, at(margin, c), at(last, c)), nv, 1)

    def down_of(slot, c):
        if slot < OWN - 1:
            return at(slot + 1, c)
        next_, margin = {OWN - 1: (0, AFTER), BEFORE: (BEFORE, 0), TAIL: (TAIL, AFTER)}.get(slot, (slot, None))
        if margin is None or (margin == AFTER and not margins):
            return jnp.where(in_last, 0.0, pltpu.roll(at(next_, c), lanes - nv, 1))
        return pltpu.roll(jnp.where(in_first, at(margin, c), at(next_, c)), lanes - nv, 1)

    for slot in slots:
        v = [at(slot, c) for c in range(comps)]
        weight = [coef[slot, kind, weight_rows, :] for kind in range(comps + 1)]
        total = weight[comps] * (v[0] + v[1] + v[2])
        for c in range(comps):
            beside = sides_of(slot, c) + (up_of(slot, c) + down_of(slot, c))
            inside = inside_of(slot)
            if inside is not None:
                beside = beside * inside
            emit(slot, c, weight[c] * v[c] + total - beside)


def operator_rows(src, coef, nv, slots, margins, inside_of, emit):
    for base in range(0, src.shape[2] - 16, 16):

        def sides_of(slot, c):
            return src[slot, c, 7 + base : 23 + base, :] + src[slot, c, 9 + base : 25 + base, :]

        def emit_rows(slot, c, value):
            emit(slot, c, base, value)

        rows, weight_rows = slice(8 + base, 24 + base), slice(base, base + 16)
        operator(src, coef, nv, rows, weight_rows, sides_of, slots, margins, inside_of, emit_rows)


def prep_kernel(own_ref, kt_ref, v0, coef, x1):
    slots, comps, cy, lanes = own_ref.shape
    own, kinds = slots - 2, comps + 1
    cx = kt_ref.shape[1] // kinds
    head = slots_of(cx)[3]
    block = iota((lanes, lanes), 1) // (lanes // H)
    for p in range(slots):
        slot = p if p < own else head + p - own
        for c in range(comps):
            v0[slot, c, 8 : 8 + cy, :] = own_ref[p, c].astype(F32)
        values = spread(kt_ref[...], row_of_slot(p, own, cx, block), kinds, cx)
        for kind, value in enumerate(terms_of(values)):
            coef[slot, kind, :cy, :] = value

    mine = [p if p < own else head + p - own for p in range(slots)]
    for slot in mine:
        v0[slot, :, :8, :] = jnp.zeros((comps, 8, lanes), F32)
        v0[slot, :, 8 + cy :, :] = jnp.zeros((comps, 8, lanes), F32)

    def emit(slot, c, base, value):
        x1[slot, c, 8 + base : 24 + base, :] = value

    operator_rows(v0, coef, lanes // H, mine, False, lambda slot: None, emit)


def fine_kernel(sizes, rank_ref, start_ref, v0_in, coef_in, x1_in, kt_ref, sec_a, sec_b, sub_a, sub_b, pack_ref, high2, low2, v0, coef, x1, x2, high3, low3, margin3):
    spans, sects = sizes
    _, comps, cy, lanes = high2.shape
    nv = start_ref.shape[1]
    cx = kt_ref.shape[1] // (comps + 1)
    OWN, BEFORE, AFTER, HEAD, TAIL = slots_of(cx)
    s, t = lax.axis_index("sub"), lax.axis_index("sec")
    sub_even, sec_even = lax.rem(s, 2) == 0, lax.rem(t, 2) == 0
    kinds = comps + 1
    low, top = slice(0, 8), slice(8 + cy, 16 + cy)
    mid = slice(8, 8 + cy)
    octets = margin_octets(sec_a, sec_b, sec_even, (OWN + 2) * comps + 1)

    def put_octet(slot, c, octet):
        v0[slot, c, low, :] = octet
        v0[slot, c, top, :] = octet

    def received(first, count):
        a, b = sub_a[first : first + count].astype(F32), sub_b[first : first + count].astype(F32)
        return jnp.where(sub_even, a, b), jnp.where(sub_even, b, a)

    narrow, parts = comps * cy, lanes // (2 * H * kinds)
    count = cy // parts
    for c in range(comps):
        for p in range(OWN + 2):
            put_octet(p if p < OWN else HEAD + p - OWN, c, octets[p * comps + c])
        v0[AFTER, c, mid, :], v0[BEFORE, c, mid, :] = received(c * cy, cy)
        after_octet, before_octet = received(narrow + count + 8 * c, 8)
        put_octet(BEFORE, c, before_octet)
        put_octet(AFTER, c, after_octet)

    octet_row = iota((8, lanes), 0)
    col_in = jnp.where(octet_row < H, jnp.where(t < sects - 1, 1.0, 0.0), jnp.where(t > 0, 1.0, 0.0))
    has_before, has_after = jnp.where(s > 0, 1.0, 0.0), jnp.where(s < spans - 1, 1.0, 0.0)
    row_in = {BEFORE: has_before, AFTER: has_after}
    octet_block = iota((8, lanes), 1) // nv
    for p in range(OWN + 2):
        slot = p if p < OWN else HEAD + p - OWN
        wanted = row_of_slot(p, OWN, cx, octet_block)
        rows = [jnp.take_along_axis(octets[-1], wanted + kind * cx, axis=1) for kind in range(kinds)]
        for kind, value in enumerate(terms_of(rows)):
            coef[slot, kind, cy : cy + 8, :] = value * col_in
    after, before = received(narrow, count)
    after_octet, before_octet = received(narrow + count + 8 * comps, 8)
    block = iota((lanes, lanes), 1) // nv
    for slot, rows, octet, side in ((AFTER, after, after_octet, 0), (BEFORE, before, before_octet, 1)):
        wide = [pltpu.roll(rows, lanes - part * 2 * H * kinds, 1) if part else rows for part in range(parts)]
        table = jnp.concatenate(wide + [octet, jnp.zeros_like(octet)], axis=0).astype(BF16)
        values = spread(table, block + side * H * kinds, kinds, H)
        for kind, value in enumerate(terms_of(values)):
            coef[slot, kind, :cy, :] = value[:cy] * row_in[slot]
            coef[slot, kind, cy : cy + 8, :] = value[cy : cy + 8] * (col_in * row_in[slot])

    everything = range(TAIL + 1)

    def apply(src, row_slots, margin_slots, emit_rows, emit_margin):
        operator_rows(src, coef, nv, row_slots, True, row_in.get, emit_rows)

        def sides_of(slot, c):
            left = jnp.where(octet_row == H, 0.0, src[slot, c, 7 + cy : 15 + cy, :])
            return left + jnp.where(octet_row == H - 1, 0.0, src[slot, c, 1:9, :])

        def inside_of(slot):
            return col_in * row_in[slot] if slot in row_in else col_in

        operator(src, coef, nv, top, slice(cy, cy + 8), sides_of, margin_slots, True, inside_of, emit_margin)

    def store(dst, split_too=False):
        def emit_rows(slot, c, base, value):
            dst[slot, c, 8 + base : 24 + base, :] = value
            if split_too and slot < HEAD:
                high2[slot, c, base : base + 16, :], low2[slot, c, base : base + 16, :] = split(value)

        def emit_margin(slot, c, value):
            dst[slot, c, low, :] = value
            dst[slot, c, top, :] = value

        return emit_rows, emit_margin

    lane = iota((16, lanes), 1)
    for c in range(comps):
        for base in range(8, 8 + cy, 16):
            rows = slice(base, base + 16)
            before = jnp.where(lane < nv, pltpu.roll(v0[BEFORE, c, rows, :], nv, 1), 0.0)
            after = jnp.where(lane >= lanes - nv, pltpu.roll(v0[AFTER, c, rows, :], lanes - nv, 1), 0.0)
            for slot, part in ((0, before), (HEAD, before), (OWN - 1, after), (TAIL, after)):
                x1[slot, c, rows, :] = x1[slot, c, rows, :] - part
        for slot in everything:
            if slot not in row_in:
                for row, beside in ((8, 7), (7 + cy, 8 + cy)):
                    x1[slot, c, row : row + 1, :] = x1[slot, c, row : row + 1, :] - v0[slot, c, beside : beside + 1, :]
    apply(v0, (BEFORE, AFTER), everything, *store(x1))
    apply(x1, everything, everything, *store(x2, True))

    def split_rows(slot, c, base, value):
        high3[slot, c, base : base + 16, :], low3[slot, c, base : base + 16, :] = split(value)

    def keep_margin(slot, c, value):
        margin3[slot, c] = value

    def fold(z):
        return sum(pltpu.roll(z[b * nv : (b + 1) * nv], (z.shape[1] - b * nv) % z.shape[1], 1) if b else z[:nv] for b in range(H))

    def flat(ref, first, count):
        return ref[first : first + count].reshape(count * comps * cy, lanes)

    chunks = range(0, AFTER + 1, 2)
    octet_margins = [x2[slot, c, top, :] for slot in range(AFTER + 1) for c in range(comps)]
    margin_h2, margin_l2 = split(jnp.concatenate(octet_margins, axis=0))

    def gram_m():
        def part(h2, l2):
            return dot(h2, jnp.concatenate([h2, l2], axis=1), TN)
        main = part(margin_h2, margin_l2)
        for first in chunks:
            main = main + part(flat(high2, first, 2), flat(low2, first, 2))
        main = fold(main)
        mixed = main[:, lanes : lanes + nv]
        return main[:, :nv] + (mixed + mixed.T)

    def gram_n():
        def part(h2, l2, h3, l3):
            return dot(h2, jnp.concatenate([h3, l3], axis=1), TN), dot(l2, h3, TN)
        h3, l3 = split(margin3[...].reshape((AFTER + 1) * comps * 8, lanes))
        main, cross = part(margin_h2, margin_l2, h3, l3)
        for first in chunks:
            more = part(*(flat(ref, first, 2) for ref in (high2, low2, high3, low3)))
            main, cross = main + more[0], cross + more[1]
        main = fold(main)
        return main[:, :nv] + main[:, lanes : lanes + nv] + fold(cross)[:, :nv]

    gram = gram_m()
    apply(x2, range(HEAD), range(HEAD), split_rows, keep_margin)
    pad = jnp.zeros((nv, lanes - nv), F32)
    inverse = inverse_factor(jnp.concatenate([gram, pad], axis=1), nv)[:, :nv]
    inverse = jnp.where(iota((nv, nv), 0) < rank_ref[0, 0], inverse, 0.0)
    image = gram_n()

    def rim(strip, first, block):
        def rows_of(slot, weighted):
            out = []
            for at, weight_at in ((mid, slice(0, cy)), (top, slice(cy, cy + 8))):
                for c in range(comps):
                    rows = x2[slot, c, at, :]
                    if weighted:
                        rows = rows * (coef[slot, c, weight_at, :] + coef[slot, comps, weight_at, :])
                    out.append(rows)
            return out

        pad = [jnp.zeros((8, lanes), F32)]
        turned = [half.T for half in split(jnp.concatenate(rows_of(strip, True) + pad, axis=0))]
        total = jnp.zeros((2 * nv, 2 * lanes), F32)
        for i in range(H):
            margin = split(jnp.concatenate([x2[first + i, c, top, :] for c in range(comps)] + pad, axis=0))
            own = [
                jnp.concatenate([ref[first + i, c] for c in range(comps)] + [rest], axis=0)
                for ref, rest in zip((high2, low2), margin)
            ]
            other = jnp.concatenate([half[i * nv : (i + 1) * nv] for half in turned], axis=0)
            total = total + dot(other, jnp.concatenate(own, axis=1), NN)
        total = total[:nv] + total[nv:]
        total = total[:, :lanes] + total[:, lanes:]
        return total[:, block * nv : (block + 1) * nv].T

    rim_next = rim(TAIL, OWN - H, H - 1) * has_after
    rim_prev = rim(HEAD, 0, 0) * has_before

    start = start_ref[...]
    k2 = start.shape[0]
    products = dot3(jnp.concatenate([inverse.T, start], axis=0), inverse, NN)
    pack_ref[0, :nv] = jnp.concatenate([rim_prev, 0.5 * image, rim_next, products[:nv]], axis=1)
    starts = [products[nv + i : nv + i + 8] for i in range(0, k2, 8)]
    pad = jnp.zeros((8, lanes - nv * len(starts)), F32)
    pack_ref[0, nv:] = jnp.concatenate(starts + [pad], axis=1)


def prolong(coefs, high_ref, low_ref, out_ref, buf, sems):
    k2, nv = coefs.shape
    comps, cx = buf.shape[0], buf.shape[2]
    cy = buf.shape[3]
    own = cx // H
    tiled = jnp.concatenate([coefs] * H, axis=1)
    tiled = jnp.broadcast_to(tiled[:, None, :], (k2, 8, H * nv)).reshape(8 * k2, H * nv)
    same = lax.rem(iota(tiled.shape, 0), 8) == iota(tiled.shape, 1) // nv
    high, low = split(jnp.where(same, tiled, 0.0))
    left = jnp.concatenate([high, low, high], axis=1)
    copies = []
    for c in range(comps):
        for p in range(own):
            bh, bl = high_ref[p, c], low_ref[p, c]
            out = dot(left, jnp.concatenate([bh, bh, bl], axis=1), NT).reshape(k2, 8, cy)
            buf[c, :, pl.ds(p, H, stride=own), :] = out[:, :H]
        copies.append(pltpu.make_async_copy(buf.at[c], out_ref.at[:, c], sems.at[c]))
        copies[-1].start()
    for copy in copies:
        copy.wait()


def level_kernel(spans, order, factor, *refs):
    parts, (high_ref, low_ref, out_ref, packs, buf, sems) = refs[:-6], refs[-6:]
    k2 = buf.shape[1]
    nv = packs.shape[1] - 8
    n = spans * nv
    s = lax.axis_index("sub")
    index = 0
    for part in parts:
        for i in range(part.shape[0]):
            packs[order[index]] = part[i]
            index += 1
    lane = iota((nv, 128), 1)

    def placed(block, offset, first, last):
        rolled = pltpu.roll(block, offset % 128, 1) if offset % 128 else block
        at = iota(block.shape, 1) - offset
        tiles = [jnp.where((at + m >= first) & (at + m < last), rolled, 0.0) for m in range(0, n, 128)]
        return jnp.concatenate(tiles, axis=1)

    rows, products = [], []
    u = jnp.zeros((k2, n), F32)
    for b in range(spans):
        pack = packs[jnp.bitwise_xor(s, b)]
        rows.append(placed(pack[:nv], nv * (b - 1), 0, 3 * nv))
        products.append(placed(pack[:nv], nv * (b - 3), 3 * nv, 4 * nv))
        starts = [placed(pack[nv:], nv * (b - i), nv * i, nv * i + nv) for i in range(k2 // 8)]
        u = u + jnp.concatenate(starts, axis=0)
    rows = jnp.concatenate(rows, axis=0)
    full = split(rows + rows.T)
    products = split(jnp.concatenate(products, axis=0))

    def times(x, halves):
        xh, xl = split(x)
        out = dot(jnp.concatenate([xh, xl], axis=0), halves[0], NN)
        return out[:k2] + (out[k2:] + dot(xh, halves[1], NN))

    z = times(times(times(u, full), products), full)
    w = times(z, products)
    gram = dot3(w, z, NT)
    gram = jnp.concatenate([gram, jnp.zeros((k2, 128 - k2), F32)], axis=1)
    own = pltpu.roll(w, lax.rem(n - nv * s, n), 1)[:, :nv]
    coefs = dot3(inverse_factor(gram, k2)[:, :k2], factor * own, NN)
    prolong(coefs, high_ref, low_ref, out_ref, buf, sems)


def pairs(count, offset):
    return [q for i in range(offset, count - 1, 2) for q in ((i, i + 1), (i + 1, i))]


def from_behind(block, axis, distance):
    devices = range(lax.axis_size(axis))
    return lax.ppermute(block, axis, [(i - distance, i) for i in devices if i - distance in devices])


def level_coefs(pack, nv, k2, factor):
    highest = lax.Precision.HIGHEST
    rim_prev, half, rim_next, product = (pack[:nv, nv * i : nv * i + nv] for i in range(4))
    u = jnp.concatenate([pack[nv:, nv * i : nv * i + nv] for i in range(k2 // 8)], axis=0).T
    own = half + half.T
    rim = rim_next + from_behind(rim_prev, "sub", -1).T
    rim_before = from_behind(rim, "sub", 1)
    for step in range(2):
        z = jnp.dot(own, u, precision=highest)
        z = z + jnp.dot(rim, from_behind(u, "sub", -1), precision=highest)
        z = z + jnp.dot(rim_before.T, from_behind(u, "sub", 1), precision=highest)
        u = jnp.dot(product, z, precision=highest)
    lower = jnp.linalg.cholesky(lax.psum(jnp.dot(z.T, u, precision=highest), "sub"))
    return factor * lax.linalg.triangular_solve(lower, u.T, left_side=True, lower=True)


def in_vmem(x):
    return pltpu.with_memory_space_constraint(x, pltpu.VMEM)


def call(kernel, out_shape, scratch, name, in_specs=None, **more):
    return pl.pallas_call(
        kernel,
        out_shape=out_shape,
        scratch_shapes=scratch,
        compiler_params=pltpu.CompilerParams(vmem_limit_bytes=VMEM_MIB * MIB),
        name=name,
        **({"in_specs": in_specs} if in_specs else {}),
        **more,
    )


def on_device(start_vectors, stiffness, coupling, kept_ranks, level_start):
    spans, sects = lax.axis_size("sub"), lax.axis_size("sec")
    nv, comps, cx, cy = start_vectors.shape
    k2 = level_start.shape[1]
    channels = comps + 1
    slots = slots_of(cx)[-1] + 1
    shape = jax.ShapeDtypeStruct
    vmem = pl.BlockSpec(memory_space=pltpu.VMEM)
    hbm = pl.BlockSpec(memory_space=pltpu.HBM)

    pieces = (cx // H + 2) * comps + 1
    inputs = (start_vectors, stiffness, coupling, level_start.T)
    sec_shape = shape((-(-pieces // 2) * 8, cy), BF16)
    own, kt, sec_a, sec_b, start, narrow = call(
        pack_kernel,
        (shape((cx // H + 2, comps, cy, H * nv), BF16), shape((cy, channels * cx), BF16), sec_shape, sec_shape)
        + (shape((k2, nv), F32), shape((2 * H * channels * cy // (H * nv), cy), BF16)),
        [
            pltpu.VMEM((comps, nv, cx, cy), BF16),
            pltpu.VMEM(stiffness.shape, BF16),
            pltpu.VMEM(coupling.shape, BF16),
            pltpu.VMEM((comps, nv * (cx + 8), cy), F32),
            pltpu.VMEM((channels * cx, cy), F32),
            pltpu.SemaphoreType.DMA((comps + 3,)),
        ],
        "pack",
        [hbm] * 4,
    )(*(pltpu.with_memory_space_constraint(x, pltpu.HBM) for x in inputs))
    sec_a = lax.ppermute(sec_a, "sec", pairs(sects, 0))
    sec_b = lax.ppermute(sec_b, "sec", pairs(sects, 1))

    def edge(*refs):
        edge_kernel(cx, *refs)

    sub_shape = shape((comps * cy + narrow.shape[0] + channels * 8, H * nv), BF16)
    sub_a, sub_b = call(edge, (sub_shape, sub_shape), [], "edge")(own, narrow, sec_a, sec_b)
    sub_a = lax.ppermute(sub_a, "sub", pairs(spans, 0))
    sub_b = lax.ppermute(sub_b, "sub", pairs(spans, 1))

    def fine(*refs):
        fine_kernel((spans, sects), *refs)

    rows = shape((slots, comps, cy + 16, H * nv), F32)
    weights = shape((slots, channels, cy + 8, H * nv), F32)
    half = shape((slots - 2, comps, cy, H * nv), BF16)
    v0, coef, x1 = (in_vmem(x) for x in call(prep_kernel, (rows, weights, rows), [], "prep")(own, kt))
    pack, high, low, *_ = call(
        fine,
        (shape((1, nv + 8, cy), F32), half, half, rows, weights, rows),
        [
            pltpu.VMEM(rows.shape, F32),
            pltpu.VMEM(half.shape, BF16),
            pltpu.VMEM(half.shape, BF16),
            pltpu.VMEM((slots - 2, comps, 8, H * nv), F32),
        ],
        "fine",
        [pl.BlockSpec(memory_space=pltpu.SMEM)] + [vmem] * 9,
        input_output_aliases={2: 3, 3: 4, 4: 5},
    )(kept_ranks, start, v0, coef, x1, kt, sec_a, sec_b, sub_a, sub_b)

    factor = math.sqrt(spans * comps * (cx + 2 * H) * (cy + 2 * H))
    result = shape((k2, comps, cx, cy), F32)
    tiles = [pltpu.VMEM((comps, k2, cx, cy), F32), pltpu.SemaphoreType.DMA((comps,))]
    if spans != 8:

        def prolong_kernel(coefs_ref, *refs):
            prolong(coefs_ref[...], *refs)

        coefs = level_coefs(pack[0], nv, k2, factor)
        return call(prolong_kernel, result, tiles, "prolong", [vmem] * 3, out_specs=hbm)(coefs, high, low)

    def swapped(block, bit):
        return lax.ppermute(block, "sub", [(i, i ^ bit) for i in range(spans)])

    far = swapped(pack, 4)
    both = jnp.concatenate([pack, far])
    parts = [both] + [swapped(both, bit) for bit in (2, 1, 3)]
    order = [high_bit ^ bit for bit in (0, 2, 1, 3) for high_bit in (0, 4)]

    def level(*refs):
        level_kernel(spans, order, factor, *refs)

    packs = pltpu.VMEM((spans,) + pack.shape[1:], F32)
    return call(level, result, [packs] + tiles, "level", [vmem] * 6, out_specs=hbm)(*parts, high, low)


def solution(mesh):
    placed = (
        P(None, None, "sub", "sec"),
        P(None, "sub", "sec"),
        P("sub", "sec"),
        P("sub", "sec"),
        P("sub", None),
    )
    return jax.shard_map(
        on_device,
        mesh=mesh,
        in_specs=placed,
        out_specs=P(None, None, "sub", "sec"),
        check_vma=False,
    )
```

```python
import math

import jax
import jax.numpy as jnp
from jax import lax
from jax.experimental import pallas as pl
from jax.experimental.pallas import tpu as pltpu
from jax.sharding import PartitionSpec as P

H = 4
MIB = 1 << 20
VMEM_MIB = 24
F32 = jnp.float32
BF16 = jnp.bfloat16
NN = (((1,), (0,)), ((), ()))
NT = (((1,), (1,)), ((), ()))
TN = (((0,), (0,)), ((), ()))


def iota(shape, dim):
    return lax.broadcasted_iota(jnp.int32, shape, dim)


def split(x):
    high = x.astype(BF16)
    return high, (x - high.astype(F32)).astype(BF16)


def dot(a, b, dims):
    return lax.dot_general(a, b, dims, preferred_element_type=F32)


def dot3(a, b, dims):
    (ah, al), (bh, bl) = split(a), split(b)
    return dot(ah, bh, dims) + (dot(ah, bl, dims) + dot(al, bh, dims))


def inverse_factor(gram, size, step=16):
    row, lane = iota((size, 128), 0), iota((size, 128), 1)
    work = jnp.where(lane < size, gram, jnp.where(lane == row + size, 1.0, 0.0))
    for first in range(0, size, step):
        columns = [jnp.broadcast_to(work[:, j : j + 1], (size, 128)) for j in range(first, first + step)]
        update = None
        for i, j in enumerate(range(first, min(first + step, size - 1))):
            factor = jnp.where(row > j, columns[i] / columns[i][j : j + 1, :], 0.0)
            for later in range(i + 1, step):
                columns[later] = columns[later] - factor * columns[later][j : j + 1, :]
            pivot = work[j : j + 1, :]
            if update is not None:
                pivot = pivot - update[j : j + 1, :]
            update = factor * pivot if update is None else update + factor * pivot
        work = work - update
    diag = jnp.sum(jnp.where(lane == row, work, 0.0), axis=1, keepdims=True)
    return pltpu.roll(work / jnp.sqrt(diag), 128 - size, 1)


def slots_of(cx):
    own = cx // H
    return own, own, own + 1, own + 2, own + 3


def halves(octet_a, octet_b):
    return jnp.where(iota(octet_a.shape, 0) < H, octet_a, octet_b)


def swap(octet):
    return pltpu.roll(octet, H, 0)


def narrowed(table, kinds, cx):
    wide = 2 * H * kinds
    parts = table.shape[1] // wide if table.shape[0] > 8 else 1
    count = table.shape[0] // parts
    lane = iota((count, table.shape[1]), 1)
    inner = lax.rem(lane, wide)
    side, kind, i = inner // (H * kinds), lax.rem(inner // H, kinds), lax.rem(inner, H)
    source = kind * cx + i + side * (cx - H)
    out = jnp.zeros((count, table.shape[1]), F32)
    for part in range(parts):
        picked = jnp.take_along_axis(table[part * count : (part + 1) * count], source, axis=1)
        out = picked if parts == 1 else jnp.where(lane // wide == part, picked, out)
    return out


def pack_kernel(
    v_hbm, k_hbm, g_hbm, start_hbm, own_ref, kt_ref, sec_a, sec_b, start_ref, narrow_ref, v_buf, k_buf, g_buf, vf, kf, sems
):
    comps, nv, cx, cy = v_buf.shape
    copies = [pltpu.make_async_copy(v_hbm.at[:, c], v_buf.at[c], sems.at[c]) for c in range(comps)]
    copies.append(pltpu.make_async_copy(k_hbm, k_buf, sems.at[comps]))
    copies.append(pltpu.make_async_copy(g_hbm, g_buf, sems.at[comps + 1]))
    copies.append(pltpu.make_async_copy(start_hbm, start_ref, sems.at[comps + 2]))
    for copy in copies:
        copy.start()
    sec_even = lax.rem(lax.axis_index("sec"), 2) == 0
    own = cx // H
    pieces = (own + 2) * comps + 1
    firsts, lasts = [None] * pieces, [None] * pieces
    for c in range(comps):
        copies[c].wait()
        for a in range(nv):
            vf[c, (cx + 8) * a : (cx + 8) * a + cx] = v_buf[c, a].astype(F32)
        for p in range(own + 2):
            rows = [b * own + p for b in range(H)] if p < own else [b + (p - own) * (cx - H) for b in range(H)]
            stack = [vf[c, pl.ds(x, nv, stride=cx + 8), :] for x in rows]
            turned = jnp.concatenate(stack, axis=0).astype(BF16).T
            own_ref[p, c] = turned
            firsts[p * comps + c] = turned[:16].astype(F32)[:8]
            lasts[p * comps + c] = turned[cy - 16 :].astype(F32)[8:]
    for copy in copies[comps:]:
        copy.wait()
    kf[: comps * cx] = k_buf[...].astype(F32).reshape(comps * cx, cy)
    kf[comps * cx :] = g_buf[...].astype(F32)
    turned = kf[...].T
    kt_ref[...] = turned.astype(BF16)
    narrow_ref[...] = narrowed(turned, comps + 1, cx).astype(BF16)
    firsts[-1], lasts[-1] = turned[:8], turned[cy - 8 :]
    for octets in (firsts, lasts):
        if len(octets) % 2:
            octets.append(jnp.zeros((8, cy), F32))
    pairs_of = range(0, len(firsts), 2)
    left = [halves(firsts[q], swap(firsts[q + 1])) for q in pairs_of]
    right = [halves(swap(lasts[q]), lasts[q + 1]) for q in pairs_of]
    left, right = jnp.concatenate(left, axis=0), jnp.concatenate(right, axis=0)
    sec_a[...] = jnp.where(sec_even, right, left).astype(BF16)
    sec_b[...] = jnp.where(sec_even, left, right).astype(BF16)


def margin_octets(sec_a, sec_b, sec_even, count):
    a, b = sec_a[...].astype(F32), sec_b[...].astype(F32)
    hi, lo = jnp.where(sec_even, a, b), jnp.where(sec_even, b, a)
    out = []
    for q in range(count):
        at = slice(8 * (q // 2), 8 * (q // 2) + 8)
        out.append(halves(swap(hi[at]), lo[at]) if q % 2 else halves(hi[at], swap(lo[at])))
    return out


def edge_kernel(cx, own_ref, narrow_ref, sec_a, sec_b, sub_a, sub_b):
    slots, comps, cy, lanes = own_ref.shape
    sub_even = lax.rem(lax.axis_index("sub"), 2) == 0
    sec_even = lax.rem(lax.axis_index("sec"), 2) == 0
    octets = margin_octets(sec_a, sec_b, sec_even, slots * comps + 1)
    first, last = slots - 2, slots - 1
    table = [narrowed(octets[-1], comps + 1, cx)]
    head = octets[first * comps : first * comps + comps] + table
    tail = octets[last * comps : last * comps + comps] + table
    head, tail = jnp.concatenate(head, axis=0), jnp.concatenate(tail, axis=0)
    for ref, to_next in ((sub_a, sub_even), (sub_b, jnp.logical_not(sub_even))):
        slot = jnp.where(to_next, last, first)
        for c in range(comps):
            ref[c * cy : (c + 1) * cy] = own_ref[slot, c]
        narrow = comps * cy + narrow_ref.shape[0]
        ref[comps * cy : narrow] = narrow_ref[...]
        ref[narrow:] = jnp.where(to_next, tail, head).astype(BF16)


def spread(table, wanted, kinds, cx):
    lanes = table.shape[1]
    source = iota((lanes, lanes), 0)
    pick = [jnp.where(source == kind * cx + wanted, 1.0, 0.0).astype(BF16) for kind in range(kinds)]
    out = dot(table, jnp.concatenate(pick, axis=1), NN)
    return [out[:, kind * lanes : (kind + 1) * lanes] for kind in range(kinds)]


def terms_of(rows):
    return [4.0 + k - rows[-1] for k in rows[:-1]] + [rows[-1]]


def row_of_slot(p, own, cx, block):
    return block * own + p if p < own else block + (p - own) * (cx - H)


def operator(src, coef, nv, rows, weight_rows, sides_of, slots, margins, inside_of, emit):
    count, comps, _, lanes = src.shape
    OWN = count - 4
    BEFORE, AFTER, HEAD, TAIL = range(OWN, count)

    def at(slot, c):
        return src[slot, c, rows, :]

    lane = iota(at(0, 0).shape, 1)
    in_first, in_last = lane < nv, lane >= lanes - nv

    def up_of(slot, c):
        if 0 < slot < OWN:
            return at(slot - 1, c)
        last, margin = {0: (OWN - 1, BEFORE), AFTER: (AFTER, OWN - 1), HEAD: (HEAD, BEFORE)}.get(slot, (slot, None))
        if margin is None or (margin == BEFORE and not margins):
            return jnp.where(in_first, 0.0, pltpu.roll(at(last, c), nv, 1))
        return pltpu.roll(jnp.where(in_last, at(margin, c), at(last, c)), nv, 1)

    def down_of(slot, c):
        if slot < OWN - 1:
            return at(slot + 1, c)
        next_, margin = {OWN - 1: (0, AFTER), BEFORE: (BEFORE, 0), TAIL: (TAIL, AFTER)}.get(slot, (slot, None))
        if margin is None or (margin == AFTER and not margins):
            return jnp.where(in_last, 0.0, pltpu.roll(at(next_, c), lanes - nv, 1))
        return pltpu.roll(jnp.where(in_first, at(margin, c), at(next_, c)), lanes - nv, 1)

    for slot in slots:
        v = [at(slot, c) for c in range(comps)]
        weight = [coef[slot, kind, weight_rows, :] for kind in range(comps + 1)]
        total = weight[comps] * (v[0] + v[1] + v[2])
        for c in range(comps):
            beside = sides_of(slot, c) + (up_of(slot, c) + down_of(slot, c))
            inside = inside_of(slot)
            if inside is not None:
                beside = beside * inside
            emit(slot, c, weight[c] * v[c] + total - beside)


def operator_rows(src, coef, nv, slots, margins, inside_of, emit):
    for base in range(0, src.shape[2] - 16, 16):

        def sides_of(slot, c):
            return src[slot, c, 7 + base : 23 + base, :] + src[slot, c, 9 + base : 25 + base, :]

        def emit_rows(slot, c, value):
            emit(slot, c, base, value)

        rows, weight_rows = slice(8 + base, 24 + base), slice(base, base + 16)
        operator(src, coef, nv, rows, weight_rows, sides_of, slots, margins, inside_of, emit_rows)


def prep_kernel(own_ref, kt_ref, v0, coef, x1):
    slots, comps, cy, lanes = own_ref.shape
    own, kinds = slots - 2, comps + 1
    cx = kt_ref.shape[1] // kinds
    head = slots_of(cx)[3]
    block = iota((lanes, lanes), 1) // (lanes // H)
    for p in range(slots):
        slot = p if p < own else head + p - own
        for c in range(comps):
            v0[slot, c, 8 : 8 + cy, :] = own_ref[p, c].astype(F32)
        values = spread(kt_ref[...], row_of_slot(p, own, cx, block), kinds, cx)
        for kind, value in enumerate(terms_of(values)):
            coef[slot, kind, :cy, :] = value

    mine = [p if p < own else head + p - own for p in range(slots)]
    for slot in mine:
        v0[slot, :, :8, :] = jnp.zeros((comps, 8, lanes), F32)
        v0[slot, :, 8 + cy :, :] = jnp.zeros((comps, 8, lanes), F32)

    def emit(slot, c, base, value):
        x1[slot, c, 8 + base : 24 + base, :] = value

    operator_rows(v0, coef, lanes // H, mine, False, lambda slot: None, emit)


def fine_kernel(sizes, rank_ref, start_ref, v0_in, coef_in, x1_in, kt_ref, sec_a, sec_b, sub_a, sub_b, pack_ref, high2, low2, v0, coef, x1, x2, twice, turned, high3, low3, margin3):
    spans, sects = sizes
    _, comps, cy, lanes = high2.shape
    nv = start_ref.shape[1]
    cx = kt_ref.shape[1] // (comps + 1)
    OWN, BEFORE, AFTER, HEAD, TAIL = slots_of(cx)
    s, t = lax.axis_index("sub"), lax.axis_index("sec")
    sub_even, sec_even = lax.rem(s, 2) == 0, lax.rem(t, 2) == 0
    kinds = comps + 1
    low, top = slice(0, 8), slice(8 + cy, 16 + cy)
    mid = slice(8, 8 + cy)
    octets = margin_octets(sec_a, sec_b, sec_even, (OWN + 2) * comps + 1)

    def put_octet(slot, c, octet):
        v0[slot, c, low, :] = octet
        v0[slot, c, top, :] = octet

    def received(first, count):
        a, b = sub_a[first : first + count].astype(F32), sub_b[first : first + count].astype(F32)
        return jnp.where(sub_even, a, b), jnp.where(sub_even, b, a)

    narrow, parts = comps * cy, lanes // (2 * H * kinds)
    count = cy // parts
    for c in range(comps):
        for p in range(OWN + 2):
            put_octet(p if p < OWN else HEAD + p - OWN, c, octets[p * comps + c])
        v0[AFTER, c, mid, :], v0[BEFORE, c, mid, :] = received(c * cy, cy)
        after_octet, before_octet = received(narrow + count + 8 * c, 8)
        put_octet(BEFORE, c, before_octet)
        put_octet(AFTER, c, after_octet)

    octet_row = iota((8, lanes), 0)
    col_in = jnp.where(octet_row < H, jnp.where(t < sects - 1, 1.0, 0.0), jnp.where(t > 0, 1.0, 0.0))
    has_before, has_after = jnp.where(s > 0, 1.0, 0.0), jnp.where(s < spans - 1, 1.0, 0.0)
    row_in = {BEFORE: has_before, AFTER: has_after}
    octet_block = iota((8, lanes), 1) // nv
    for p in range(OWN + 2):
        slot = p if p < OWN else HEAD + p - OWN
        wanted = row_of_slot(p, OWN, cx, octet_block)
        rows = [jnp.take_along_axis(octets[-1], wanted + kind * cx, axis=1) for kind in range(kinds)]
        for kind, value in enumerate(terms_of(rows)):
            coef[slot, kind, cy : cy + 8, :] = value * col_in
    after, before = received(narrow, count)
    after_octet, before_octet = received(narrow + count + 8 * comps, 8)
    block = iota((lanes, lanes), 1) // nv
    for slot, rows, octet, side in ((AFTER, after, after_octet, 0), (BEFORE, before, before_octet, 1)):
        wide = [pltpu.roll(rows, lanes - part * 2 * H * kinds, 1) if part else rows for part in range(parts)]
        table = jnp.concatenate(wide + [octet, jnp.zeros_like(octet)], axis=0).astype(BF16)
        values = spread(table, block + side * H * kinds, kinds, H)
        for kind, value in enumerate(terms_of(values)):
            coef[slot, kind, :cy, :] = value[:cy] * row_in[slot]
            coef[slot, kind, cy : cy + 8, :] = value[cy : cy + 8] * (col_in * row_in[slot])

    everything = range(TAIL + 1)

    def apply(src, row_slots, margin_slots, emit_rows, emit_margin):
        operator_rows(src, coef, nv, row_slots, True, row_in.get, emit_rows)

        def sides_of(slot, c):
            left = jnp.where(octet_row == H, 0.0, src[slot, c, 7 + cy : 15 + cy, :])
            return left + jnp.where(octet_row == H - 1, 0.0, src[slot, c, 1:9, :])

        def inside_of(slot):
            return col_in * row_in[slot] if slot in row_in else col_in

        operator(src, coef, nv, top, slice(cy, cy + 8), sides_of, margin_slots, True, inside_of, emit_margin)

    def put_margin(dst, slot, c, value):
        dst[slot, c, low, :] = value
        dst[slot, c, top, :] = value

    def store_rows(slot, c, base, value):
        x1[slot, c, 8 + base : 24 + base, :] = value

    def store_margin(slot, c, value):
        put_margin(x1, slot, c, value)

    def residual(value):
        return value - value.astype(BF16).astype(F32)

    def split_rows(slot, c, base, value):
        rows = slice(8 + base, 24 + base)
        if slot < HEAD:
            rest = residual(value)
            high2[slot, c, base : base + 16, :], low2[slot, c, base : base + 16, :] = value.astype(BF16), rest.astype(BF16)
            twice[slot, c, rows, :] = value + rest
        else:
            x2[slot, c, rows, :] = value

    def split_margin(slot, c, value):
        x2[slot, c, top, :] = value
        if slot < HEAD:
            put_margin(twice, slot, c, value + residual(value))

    lane = iota((16, lanes), 1)
    for c in range(comps):
        for base in range(8, 8 + cy, 16):
            rows = slice(base, base + 16)
            before = jnp.where(lane < nv, pltpu.roll(v0[BEFORE, c, rows, :], nv, 1), 0.0)
            after = jnp.where(lane >= lanes - nv, pltpu.roll(v0[AFTER, c, rows, :], lanes - nv, 1), 0.0)
            for slot, part in ((0, before), (HEAD, before), (OWN - 1, after), (TAIL, after)):
                x1[slot, c, rows, :] = x1[slot, c, rows, :] - part
        for slot in everything:
            if slot not in row_in:
                for row, beside in ((8, 7), (7 + cy, 8 + cy)):
                    x1[slot, c, row : row + 1, :] = x1[slot, c, row : row + 1, :] - v0[slot, c, beside : beside + 1, :]
    apply(v0, (BEFORE, AFTER), everything, store_rows, store_margin)
    apply(x1, everything, everything, split_rows, split_margin)

    def image_rows(slot, c, base, value):
        high3[slot, c, base : base + 16, :], low3[slot, c, base : base + 16, :] = split(value)

    def keep_margin(slot, c, value):
        margin3[slot, c] = value

    def fold(z):
        return sum(pltpu.roll(z[b * nv : (b + 1) * nv], (z.shape[1] - b * nv) % z.shape[1], 1) if b else z[:nv] for b in range(H))

    def flat(ref, first, count):
        return ref[first : first + count].reshape(count * comps * cy, lanes)

    chunks = range(0, AFTER + 1, 2)
    octet_margins = [x2[slot, c, top, :] for slot in range(AFTER + 1) for c in range(comps)]
    margin_h2, margin_l2 = split(jnp.concatenate(octet_margins, axis=0))

    def product(other):
        margin, rows = other
        main = dot(margin_h2, jnp.concatenate(margin, axis=1), TN)
        for first in chunks:
            both = jnp.concatenate([flat(ref, first, 2) for ref in rows], axis=1)
            main = main + dot(turned[first // 2], both, NN)
        main = fold(main)
        return main[:, :nv], main[:, lanes : lanes + nv]

    def gram_m():
        for first in chunks:
            turned[first // 2] = flat(high2, first, 2).T
        main, mixed = product(((margin_h2, margin_l2), (high2, low2)))
        return main + (mixed + mixed.T)

    def gram_n():
        margin = split(margin3[...].reshape((AFTER + 1) * comps * 8, lanes))
        out = sum(product((margin, (high3, low3))))
        return 0.5 * (out + out.T)

    gram = gram_m()
    apply(twice, range(HEAD), range(HEAD), image_rows, keep_margin)
    pad = jnp.zeros((nv, lanes - nv), F32)
    inverse = inverse_factor(jnp.concatenate([gram, pad], axis=1), nv)[:, :nv]
    inverse = jnp.where(iota((nv, nv), 0) < rank_ref[0, 0], inverse, 0.0)
    image = gram_n()

    def rim(strip, first, block):
        def rows_of(slot, weighted):
            out = []
            for at, weight_at in ((mid, slice(0, cy)), (top, slice(cy, cy + 8))):
                for c in range(comps):
                    rows = x2[slot, c, at, :]
                    if weighted:
                        rows = rows * (coef[slot, c, weight_at, :] + coef[slot, comps, weight_at, :])
                    out.append(rows)
            return out

        pad = [jnp.zeros((8, lanes), F32)]
        turned = [half.T for half in split(jnp.concatenate(rows_of(strip, True) + pad, axis=0))]
        total = jnp.zeros((2 * nv, 2 * lanes), F32)
        for i in range(H):
            margin = split(jnp.concatenate([x2[first + i, c, top, :] for c in range(comps)] + pad, axis=0))
            own = [
                jnp.concatenate([ref[first + i, c] for c in range(comps)] + [rest], axis=0)
                for ref, rest in zip((high2, low2), margin)
            ]
            other = jnp.concatenate([half[i * nv : (i + 1) * nv] for half in turned], axis=0)
            total = total + dot(other, jnp.concatenate(own, axis=1), NN)
        total = total[:nv] + total[nv:]
        total = total[:, :lanes] + total[:, lanes:]
        return total[:, block * nv : (block + 1) * nv].T

    rim_next = rim(TAIL, OWN - H, H - 1) * has_after
    rim_prev = rim(HEAD, 0, 0) * has_before

    start = start_ref[...]
    k2 = start.shape[0]
    products = dot3(jnp.concatenate([inverse.T, start], axis=0), inverse, NN)
    pack_ref[0, :nv] = jnp.concatenate([rim_prev, 0.5 * image, rim_next, products[:nv]], axis=1)
    starts = [products[nv + i : nv + i + 8] for i in range(0, k2, 8)]
    pad = jnp.zeros((8, lanes - nv * len(starts)), F32)
    pack_ref[0, nv:] = jnp.concatenate(starts + [pad], axis=1)


def prolong(coefs, high_ref, low_ref, out_ref, buf, sems):
    k2, nv = coefs.shape
    comps, cx = buf.shape[0], buf.shape[2]
    cy = buf.shape[3]
    own = cx // H
    tiled = jnp.concatenate([coefs] * H, axis=1)
    tiled = jnp.broadcast_to(tiled[:, None, :], (k2, 8, H * nv)).reshape(8 * k2, H * nv)
    same = lax.rem(iota(tiled.shape, 0), 8) == iota(tiled.shape, 1) // nv
    high, low = split(jnp.where(same, tiled, 0.0))
    left = jnp.concatenate([high, low, high], axis=1)
    copies = []
    for c in range(comps):
        for p in range(own):
            bh, bl = high_ref[p, c], low_ref[p, c]
            out = dot(left, jnp.concatenate([bh, bh, bl], axis=1), NT).reshape(k2, 8, cy)
            buf[c, :, pl.ds(p, H, stride=own), :] = out[:, :H]
        copies.append(pltpu.make_async_copy(buf.at[c], out_ref.at[:, c], sems.at[c]))
        copies[-1].start()
    for copy in copies:
        copy.wait()


def level_kernel(spans, order, factor, *refs):
    parts, (high_ref, low_ref, out_ref, packs, buf, sems) = refs[:-6], refs[-6:]
    k2 = buf.shape[1]
    nv = packs.shape[1] - 8
    n = spans * nv
    s = lax.axis_index("sub")
    index = 0
    for part in parts:
        for i in range(part.shape[0]):
            packs[order[index]] = part[i]
            index += 1
    lane = iota((nv, 128), 1)

    def placed(block, offset, first, last):
        rolled = pltpu.roll(block, offset % 128, 1) if offset % 128 else block
        at = iota(block.shape, 1) - offset
        tiles = [jnp.where((at + m >= first) & (at + m < last), rolled, 0.0) for m in range(0, n, 128)]
        return jnp.concatenate(tiles, axis=1)

    rows, products = [], []
    u = jnp.zeros((k2, n), F32)
    for b in range(spans):
        pack = packs[jnp.bitwise_xor(s, b)]
        rows.append(placed(pack[:nv], nv * (b - 1), 0, 3 * nv))
        products.append(placed(pack[:nv], nv * (b - 3), 3 * nv, 4 * nv))
        starts = [placed(pack[nv:], nv * (b - i), nv * i, nv * i + nv) for i in range(k2 // 8)]
        u = u + jnp.concatenate(starts, axis=0)
    rows = jnp.concatenate(rows, axis=0)
    full = split(rows + rows.T)
    products = split(jnp.concatenate(products, axis=0))

    def times(x, halves):
        xh, xl = split(x)
        out = dot(jnp.concatenate([xh, xl], axis=0), halves[0], NN)
        return out[:k2] + (out[k2:] + dot(xh, halves[1], NN))

    z = times(times(times(u, full), products), full)
    w = times(z, products)
    gram = dot3(w, z, NT)
    gram = jnp.concatenate([gram, jnp.zeros((k2, 128 - k2), F32)], axis=1)
    own = pltpu.roll(w, lax.rem(n - nv * s, n), 1)[:, :nv]
    coefs = dot3(inverse_factor(gram, k2)[:, :k2], factor * own, NN)
    prolong(coefs, high_ref, low_ref, out_ref, buf, sems)


def pairs(count, offset):
    return [q for i in range(offset, count - 1, 2) for q in ((i, i + 1), (i + 1, i))]


def from_behind(block, axis, distance):
    devices = range(lax.axis_size(axis))
    return lax.ppermute(block, axis, [(i - distance, i) for i in devices if i - distance in devices])


def level_coefs(pack, nv, k2, factor):
    highest = lax.Precision.HIGHEST
    rim_prev, half, rim_next, product = (pack[:nv, nv * i : nv * i + nv] for i in range(4))
    u = jnp.concatenate([pack[nv:, nv * i : nv * i + nv] for i in range(k2 // 8)], axis=0).T
    own = half + half.T
    rim = rim_next + from_behind(rim_prev, "sub", -1).T
    rim_before = from_behind(rim, "sub", 1)
    for step in range(2):
        z = jnp.dot(own, u, precision=highest)
        z = z + jnp.dot(rim, from_behind(u, "sub", -1), precision=highest)
        z = z + jnp.dot(rim_before.T, from_behind(u, "sub", 1), precision=highest)
        u = jnp.dot(product, z, precision=highest)
    lower = jnp.linalg.cholesky(lax.psum(jnp.dot(z.T, u, precision=highest), "sub"))
    return factor * lax.linalg.triangular_solve(lower, u.T, left_side=True, lower=True)


def in_vmem(x):
    return pltpu.with_memory_space_constraint(x, pltpu.VMEM)


def call(kernel, out_shape, scratch, name, in_specs=None, **more):
    return pl.pallas_call(
        kernel,
        out_shape=out_shape,
        scratch_shapes=scratch,
        compiler_params=pltpu.CompilerParams(vmem_limit_bytes=VMEM_MIB * MIB),
        name=name,
        **({"in_specs": in_specs} if in_specs else {}),
        **more,
    )


def on_device(start_vectors, stiffness, coupling, kept_ranks, level_start):
    spans, sects = lax.axis_size("sub"), lax.axis_size("sec")
    nv, comps, cx, cy = start_vectors.shape
    k2 = level_start.shape[1]
    channels = comps + 1
    slots = slots_of(cx)[-1] + 1
    shape = jax.ShapeDtypeStruct
    vmem = pl.BlockSpec(memory_space=pltpu.VMEM)
    hbm = pl.BlockSpec(memory_space=pltpu.HBM)

    pieces = (cx // H + 2) * comps + 1
    inputs = (start_vectors, stiffness, coupling, level_start.T)
    sec_shape = shape((-(-pieces // 2) * 8, cy), BF16)
    own, kt, sec_a, sec_b, start, narrow = call(
        pack_kernel,
        (shape((cx // H + 2, comps, cy, H * nv), BF16), shape((cy, channels * cx), BF16), sec_shape, sec_shape)
        + (shape((k2, nv), F32), shape((2 * H * channels * cy // (H * nv), cy), BF16)),
        [
            pltpu.VMEM((comps, nv, cx, cy), BF16),
            pltpu.VMEM(stiffness.shape, BF16),
            pltpu.VMEM(coupling.shape, BF16),
            pltpu.VMEM((comps, nv * (cx + 8), cy), F32),
            pltpu.VMEM((channels * cx, cy), F32),
            pltpu.SemaphoreType.DMA((comps + 3,)),
        ],
        "pack",
        [hbm] * 4,
    )(*(pltpu.with_memory_space_constraint(x, pltpu.HBM) for x in inputs))
    sec_a = lax.ppermute(sec_a, "sec", pairs(sects, 0))
    sec_b = lax.ppermute(sec_b, "sec", pairs(sects, 1))

    def edge(*refs):
        edge_kernel(cx, *refs)

    sub_shape = shape((comps * cy + narrow.shape[0] + channels * 8, H * nv), BF16)
    sub_a, sub_b = call(edge, (sub_shape, sub_shape), [], "edge")(own, narrow, sec_a, sec_b)
    sub_a = lax.ppermute(sub_a, "sub", pairs(spans, 0))
    sub_b = lax.ppermute(sub_b, "sub", pairs(spans, 1))

    def fine(*refs):
        fine_kernel((spans, sects), *refs)

    rows = shape((slots, comps, cy + 16, H * nv), F32)
    weights = shape((slots, channels, cy + 8, H * nv), F32)
    half = shape((slots - 2, comps, cy, H * nv), BF16)
    v0, coef, x1 = (in_vmem(x) for x in call(prep_kernel, (rows, weights, rows), [], "prep")(own, kt))
    pack, high, low, *_ = call(
        fine,
        (shape((1, nv + 8, cy), F32), half, half, rows, weights, rows),
        [
            pltpu.VMEM(rows.shape, F32),
            pltpu.VMEM(rows.shape, F32),
            pltpu.VMEM(((slots - 2) // 2, H * nv, 2 * comps * cy), BF16),
            pltpu.VMEM(half.shape, BF16),
            pltpu.VMEM(half.shape, BF16),
            pltpu.VMEM((slots - 2, comps, 8, H * nv), F32),
        ],
        "fine",
        [pl.BlockSpec(memory_space=pltpu.SMEM)] + [vmem] * 9,
        input_output_aliases={2: 3, 3: 4, 4: 5},
    )(kept_ranks, start, v0, coef, x1, kt, sec_a, sec_b, sub_a, sub_b)

    factor = math.sqrt(spans * comps * (cx + 2 * H) * (cy + 2 * H))
    result = shape((k2, comps, cx, cy), F32)
    tiles = [pltpu.VMEM((comps, k2, cx, cy), F32), pltpu.SemaphoreType.DMA((comps,))]
    if spans != 8:

        def prolong_kernel(coefs_ref, *refs):
            prolong(coefs_ref[...], *refs)

        coefs = level_coefs(pack[0], nv, k2, factor)
        return call(prolong_kernel, result, tiles, "prolong", [vmem] * 3, out_specs=hbm)(coefs, high, low)

    def swapped(block, bit):
        return lax.ppermute(block, "sub", [(i, i ^ bit) for i in range(spans)])

    far = swapped(pack, 4)
    both = jnp.concatenate([pack, far])
    parts = [both] + [swapped(both, bit) for bit in (2, 1, 3)]
    order = [high_bit ^ bit for bit in (0, 2, 1, 3) for high_bit in (0, 4)]

    def level(*refs):
        level_kernel(spans, order, factor, *refs)

    packs = pltpu.VMEM((spans,) + pack.shape[1:], F32)
    return call(level, result, [packs] + tiles, "level", [vmem] * 6, out_specs=hbm)(*parts, high, low)


def solution(mesh):
    placed = (
        P(None, None, "sub", "sec"),
        P(None, "sub", "sec"),
        P("sub", "sec"),
        P("sub", "sec"),
        P("sub", None),
    )
    return jax.shard_map(
        on_device,
        mesh=mesh,
        in_specs=placed,
        out_specs=P(None, None, "sub", "sec"),
        check_vma=False,
    )
```

```python
import math

import jax
import jax.numpy as jnp
from jax import lax
from jax.experimental import pallas as pl
from jax.experimental.pallas import tpu as pltpu
from jax.sharding import PartitionSpec as P

H = 4
MIB = 1 << 20
VMEM_MIB = 24
F32 = jnp.float32
BF16 = jnp.bfloat16
NN = (((1,), (0,)), ((), ()))
NT = (((1,), (1,)), ((), ()))
TN = (((0,), (0,)), ((), ()))


def iota(shape, dim):
    return lax.broadcasted_iota(jnp.int32, shape, dim)


def split(x):
    high = x.astype(BF16)
    return high, (x - high.astype(F32)).astype(BF16)


def dot(a, b, dims):
    return lax.dot_general(a, b, dims, preferred_element_type=F32)


def dot3(a, b, dims):
    (ah, al), (bh, bl) = split(a), split(b)
    return dot(ah, bh, dims) + (dot(ah, bl, dims) + dot(al, bh, dims))


def inverse_factor(gram, size, step):
    row, lane = iota((size, 128), 0), iota((size, 128), 1)
    work = jnp.where(lane < size, gram, jnp.where(lane == row + size, 1.0, 0.0))
    for first in range(0, size, step):
        columns = [jnp.broadcast_to(work[:, j : j + 1], (size, 128)) for j in range(first, first + step)]
        update = None
        for i, j in enumerate(range(first, min(first + step, size - 1))):
            factor = jnp.where(row > j, columns[i] / columns[i][j : j + 1, :], 0.0)
            for later in range(i + 1, step):
                columns[later] = columns[later] - factor * columns[later][j : j + 1, :]
            pivot = work[j : j + 1, :]
            if update is not None:
                pivot = pivot - update[j : j + 1, :]
            update = factor * pivot if update is None else update + factor * pivot
        work = work - update
    diag = jnp.sum(jnp.where(lane == row, work, 0.0), axis=1, keepdims=True)
    return pltpu.roll(work / jnp.sqrt(diag), 128 - size, 1)


def slots_of(cx):
    own = cx // H
    return own, own, own + 1, own + 2, own + 3


def halves(octet_a, octet_b):
    return jnp.where(iota(octet_a.shape, 0) < H, octet_a, octet_b)


def swap(octet):
    return pltpu.roll(octet, H, 0)


def narrowed(table, kinds, cx):
    wide = 2 * H * kinds
    parts = table.shape[1] // wide if table.shape[0] > 8 else 1
    count = table.shape[0] // parts
    lane = iota((count, table.shape[1]), 1)
    inner = lax.rem(lane, wide)
    side, kind, i = inner // (H * kinds), lax.rem(inner // H, kinds), lax.rem(inner, H)
    source = kind * cx + i + side * (cx - H)
    out = jnp.zeros((count, table.shape[1]), F32)
    for part in range(parts):
        picked = jnp.take_along_axis(table[part * count : (part + 1) * count], source, axis=1)
        out = picked if parts == 1 else jnp.where(lane // wide == part, picked, out)
    return out


def pack_kernel(
    v_hbm, k_hbm, g_hbm, start_hbm, own_ref, kt_ref, sec_a, sec_b, start_ref, narrow_ref, v_buf, k_buf, g_buf, vf, kf, sems
):
    comps, nv, cx, cy = v_buf.shape
    copies = [pltpu.make_async_copy(v_hbm.at[:, c], v_buf.at[c], sems.at[c]) for c in range(comps)]
    copies.append(pltpu.make_async_copy(k_hbm, k_buf, sems.at[comps]))
    copies.append(pltpu.make_async_copy(g_hbm, g_buf, sems.at[comps + 1]))
    copies.append(pltpu.make_async_copy(start_hbm, start_ref, sems.at[comps + 2]))
    for copy in copies:
        copy.start()
    sec_even = lax.rem(lax.axis_index("sec"), 2) == 0
    own = cx // H
    pieces = (own + 2) * comps + 1
    firsts, lasts = [None] * pieces, [None] * pieces
    for c in range(comps):
        copies[c].wait()
        for a in range(nv):
            vf[c, (cx + 8) * a : (cx + 8) * a + cx] = v_buf[c, a].astype(F32)
        for p in range(own + 2):
            rows = [b * own + p for b in range(H)] if p < own else [b + (p - own) * (cx - H) for b in range(H)]
            stack = [vf[c, pl.ds(x, nv, stride=cx + 8), :] for x in rows]
            turned = jnp.concatenate(stack, axis=0).astype(BF16).T
            own_ref[p, c] = turned
            firsts[p * comps + c] = turned[:16].astype(F32)[:8]
            lasts[p * comps + c] = turned[cy - 16 :].astype(F32)[8:]
    for copy in copies[comps:]:
        copy.wait()
    kf[: comps * cx] = k_buf[...].astype(F32).reshape(comps * cx, cy)
    kf[comps * cx :] = g_buf[...].astype(F32)
    turned = kf[...].T
    kt_ref[...] = turned.astype(BF16)
    narrow_ref[...] = narrowed(turned, comps + 1, cx).astype(BF16)
    firsts[-1], lasts[-1] = turned[:8], turned[cy - 8 :]
    for octets in (firsts, lasts):
        if len(octets) % 2:
            octets.append(jnp.zeros((8, cy), F32))
    pairs_of = range(0, len(firsts), 2)
    left = [halves(firsts[q], swap(firsts[q + 1])) for q in pairs_of]
    right = [halves(swap(lasts[q]), lasts[q + 1]) for q in pairs_of]
    left, right = jnp.concatenate(left, axis=0), jnp.concatenate(right, axis=0)
    sec_a[...] = jnp.where(sec_even, right, left).astype(BF16)
    sec_b[...] = jnp.where(sec_even, left, right).astype(BF16)


def margin_octets(sec_a, sec_b, sec_even, count):
    a, b = sec_a[...].astype(F32), sec_b[...].astype(F32)
    hi, lo = jnp.where(sec_even, a, b), jnp.where(sec_even, b, a)
    out = []
    for q in range(count):
        at = slice(8 * (q // 2), 8 * (q // 2) + 8)
        out.append(halves(swap(hi[at]), lo[at]) if q % 2 else halves(hi[at], swap(lo[at])))
    return out


def edge_kernel(cx, own_ref, narrow_ref, sec_a, sec_b, sub_a, sub_b):
    slots, comps, cy, lanes = own_ref.shape
    sub_even = lax.rem(lax.axis_index("sub"), 2) == 0
    sec_even = lax.rem(lax.axis_index("sec"), 2) == 0
    octets = margin_octets(sec_a, sec_b, sec_even, slots * comps + 1)
    first, last = slots - 2, slots - 1
    table = [narrowed(octets[-1], comps + 1, cx)]
    head = octets[first * comps : first * comps + comps] + table
    tail = octets[last * comps : last * comps + comps] + table
    head, tail = jnp.concatenate(head, axis=0), jnp.concatenate(tail, axis=0)
    for ref, to_next in ((sub_a, sub_even), (sub_b, jnp.logical_not(sub_even))):
        slot = jnp.where(to_next, last, first)
        for c in range(comps):
            ref[c * cy : (c + 1) * cy] = own_ref[slot, c]
        narrow = comps * cy + narrow_ref.shape[0]
        ref[comps * cy : narrow] = narrow_ref[...]
        ref[narrow:] = jnp.where(to_next, tail, head).astype(BF16)


def spread(table, wanted, kinds, cx):
    lanes = table.shape[1]
    source = iota((lanes, lanes), 0)
    pick = [jnp.where(source == kind * cx + wanted, 1.0, 0.0).astype(BF16) for kind in range(kinds)]
    out = dot(table, jnp.concatenate(pick, axis=1), NN)
    return [out[:, kind * lanes : (kind + 1) * lanes] for kind in range(kinds)]


def terms_of(rows):
    return [4.0 + k - rows[-1] for k in rows[:-1]] + [rows[-1]]


def row_of_slot(p, own, cx, block):
    return block * own + p if p < own else block + (p - own) * (cx - H)


def operator(src, coef, nv, rows, weight_rows, sides_of, slots, margins, inside_of, emit):
    count, comps, _, lanes = src.shape
    OWN = count - 4
    BEFORE, AFTER, HEAD, TAIL = range(OWN, count)

    def at(slot, c):
        return src[slot, c, rows, :]

    lane = iota(at(0, 0).shape, 1)
    in_first, in_last = lane < nv, lane >= lanes - nv

    def up_of(slot, c):
        if 0 < slot < OWN:
            return at(slot - 1, c)
        last, margin = {0: (OWN - 1, BEFORE), AFTER: (AFTER, OWN - 1), HEAD: (HEAD, BEFORE)}.get(slot, (slot, None))
        if margin is None or (margin == BEFORE and not margins):
            return jnp.where(in_first, 0.0, pltpu.roll(at(last, c), nv, 1))
        return pltpu.roll(jnp.where(in_last, at(margin, c), at(last, c)), nv, 1)

    def down_of(slot, c):
        if slot < OWN - 1:
            return at(slot + 1, c)
        next_, margin = {OWN - 1: (0, AFTER), BEFORE: (BEFORE, 0), TAIL: (TAIL, AFTER)}.get(slot, (slot, None))
        if margin is None or (margin == AFTER and not margins):
            return jnp.where(in_last, 0.0, pltpu.roll(at(next_, c), lanes - nv, 1))
        return pltpu.roll(jnp.where(in_first, at(margin, c), at(next_, c)), lanes - nv, 1)

    for slot in slots:
        v = [at(slot, c) for c in range(comps)]
        weight = [coef[slot, kind, weight_rows, :] for kind in range(comps + 1)]
        total = weight[comps] * (v[0] + v[1] + v[2])
        for c in range(comps):
            beside = sides_of(slot, c) + (up_of(slot, c) + down_of(slot, c))
            inside = inside_of(slot)
            if inside is not None:
                beside = beside * inside
            emit(slot, c, weight[c] * v[c] + total - beside)


def operator_rows(src, coef, nv, slots, margins, inside_of, emit):
    for base in range(0, src.shape[2] - 16, 16):

        def sides_of(slot, c):
            return src[slot, c, 7 + base : 23 + base, :] + src[slot, c, 9 + base : 25 + base, :]

        def emit_rows(slot, c, value):
            emit(slot, c, base, value)

        rows, weight_rows = slice(8 + base, 24 + base), slice(base, base + 16)
        operator(src, coef, nv, rows, weight_rows, sides_of, slots, margins, inside_of, emit_rows)


def prep_kernel(own_ref, kt_ref, v0, coef, x1):
    slots, comps, cy, lanes = own_ref.shape
    own, kinds = slots - 2, comps + 1
    cx = kt_ref.shape[1] // kinds
    head = slots_of(cx)[3]
    block = iota((lanes, lanes), 1) // (lanes // H)
    for p in range(slots):
        slot = p if p < own else head + p - own
        for c in range(comps):
            v0[slot, c, 8 : 8 + cy, :] = own_ref[p, c].astype(F32)
        values = spread(kt_ref[...], row_of_slot(p, own, cx, block), kinds, cx)
        for kind, value in enumerate(terms_of(values)):
            coef[slot, kind, :cy, :] = value

    mine = [p if p < own else head + p - own for p in range(slots)]
    for slot in mine:
        v0[slot, :, :8, :] = jnp.zeros((comps, 8, lanes), F32)
        v0[slot, :, 8 + cy :, :] = jnp.zeros((comps, 8, lanes), F32)

    def emit(slot, c, base, value):
        x1[slot, c, 8 + base : 24 + base, :] = value

    operator_rows(v0, coef, lanes // H, mine, False, lambda slot: None, emit)


def fine_kernel(sizes, rank_ref, start_ref, v0_in, coef_in, x1_in, kt_ref, sec_a, sec_b, sub_a, sub_b, pack_ref, high2, low2, v0, coef, x1, x2, twice, turned, high3, low3, margin3):
    spans, sects = sizes
    _, comps, cy, lanes = high2.shape
    nv = start_ref.shape[1]
    cx = kt_ref.shape[1] // (comps + 1)
    OWN, BEFORE, AFTER, HEAD, TAIL = slots_of(cx)
    s, t = lax.axis_index("sub"), lax.axis_index("sec")
    sub_even, sec_even = lax.rem(s, 2) == 0, lax.rem(t, 2) == 0
    kinds = comps + 1
    low, top = slice(0, 8), slice(8 + cy, 16 + cy)
    mid = slice(8, 8 + cy)
    octets = margin_octets(sec_a, sec_b, sec_even, (OWN + 2) * comps + 1)

    def put_octet(slot, c, octet):
        v0[slot, c, low, :] = octet
        v0[slot, c, top, :] = octet

    def received(first, count):
        a, b = sub_a[first : first + count].astype(F32), sub_b[first : first + count].astype(F32)
        return jnp.where(sub_even, a, b), jnp.where(sub_even, b, a)

    narrow, parts = comps * cy, lanes // (2 * H * kinds)
    count = cy // parts
    for c in range(comps):
        for p in range(OWN + 2):
            put_octet(p if p < OWN else HEAD + p - OWN, c, octets[p * comps + c])
        v0[AFTER, c, mid, :], v0[BEFORE, c, mid, :] = received(c * cy, cy)
        after_octet, before_octet = received(narrow + count + 8 * c, 8)
        put_octet(BEFORE, c, before_octet)
        put_octet(AFTER, c, after_octet)

    octet_row = iota((8, lanes), 0)
    col_in = jnp.where(octet_row < H, jnp.where(t < sects - 1, 1.0, 0.0), jnp.where(t > 0, 1.0, 0.0))
    has_before, has_after = jnp.where(s > 0, 1.0, 0.0), jnp.where(s < spans - 1, 1.0, 0.0)
    row_in = {BEFORE: has_before, AFTER: has_after}
    octet_block = iota((8, lanes), 1) // nv
    for p in range(OWN + 2):
        slot = p if p < OWN else HEAD + p - OWN
        wanted = row_of_slot(p, OWN, cx, octet_block)
        rows = [jnp.take_along_axis(octets[-1], wanted + kind * cx, axis=1) for kind in range(kinds)]
        for kind, value in enumerate(terms_of(rows)):
            coef[slot, kind, cy : cy + 8, :] = value * col_in
    after, before = received(narrow, count)
    after_octet, before_octet = received(narrow + count + 8 * comps, 8)
    block = iota((lanes, lanes), 1) // nv
    for slot, rows, octet, side in ((AFTER, after, after_octet, 0), (BEFORE, before, before_octet, 1)):
        wide = [pltpu.roll(rows, lanes - part * 2 * H * kinds, 1) if part else rows for part in range(parts)]
        table = jnp.concatenate(wide + [octet, jnp.zeros_like(octet)], axis=0).astype(BF16)
        values = spread(table, block + side * H * kinds, kinds, H)
        for kind, value in enumerate(terms_of(values)):
            coef[slot, kind, :cy, :] = value[:cy] * row_in[slot]
            coef[slot, kind, cy : cy + 8, :] = value[cy : cy + 8] * (col_in * row_in[slot])

    everything = range(TAIL + 1)

    def apply(src, row_slots, margin_slots, emit_rows, emit_margin):
        operator_rows(src, coef, nv, row_slots, True, row_in.get, emit_rows)

        def sides_of(slot, c):
            left = jnp.where(octet_row == H, 0.0, src[slot, c, 7 + cy : 15 + cy, :])
            return left + jnp.where(octet_row == H - 1, 0.0, src[slot, c, 1:9, :])

        def inside_of(slot):
            return col_in * row_in[slot] if slot in row_in else col_in

        operator(src, coef, nv, top, slice(cy, cy + 8), sides_of, margin_slots, True, inside_of, emit_margin)

    def put_margin(dst, slot, c, value):
        dst[slot, c, low, :] = value
        dst[slot, c, top, :] = value

    def store_rows(slot, c, base, value):
        x1[slot, c, 8 + base : 24 + base, :] = value

    def store_margin(slot, c, value):
        put_margin(x1, slot, c, value)

    def residual(value):
        return value - value.astype(BF16).astype(F32)

    def split_rows(slot, c, base, value):
        rows = slice(8 + base, 24 + base)
        if slot < HEAD:
            rest = residual(value)
            high2[slot, c, base : base + 16, :], low2[slot, c, base : base + 16, :] = value.astype(BF16), rest.astype(BF16)
            twice[slot, c, rows, :] = value + rest
        else:
            x2[slot, c, rows, :] = value

    def split_margin(slot, c, value):
        x2[slot, c, top, :] = value
        if slot < HEAD:
            put_margin(twice, slot, c, value + residual(value))

    lane = iota((16, lanes), 1)
    for c in range(comps):
        for base in range(8, 8 + cy, 16):
            rows = slice(base, base + 16)
            before = jnp.where(lane < nv, pltpu.roll(v0[BEFORE, c, rows, :], nv, 1), 0.0)
            after = jnp.where(lane >= lanes - nv, pltpu.roll(v0[AFTER, c, rows, :], lanes - nv, 1), 0.0)
            for slot, part in ((0, before), (HEAD, before), (OWN - 1, after), (TAIL, after)):
                x1[slot, c, rows, :] = x1[slot, c, rows, :] - part
        for slot in everything:
            if slot not in row_in:
                for row, beside in ((8, 7), (7 + cy, 8 + cy)):
                    x1[slot, c, row : row + 1, :] = x1[slot, c, row : row + 1, :] - v0[slot, c, beside : beside + 1, :]
    apply(v0, (BEFORE, AFTER), everything, store_rows, store_margin)
    apply(x1, everything, everything, split_rows, split_margin)

    def image_rows(slot, c, base, value):
        high3[slot, c, base : base + 16, :], low3[slot, c, base : base + 16, :] = split(value)

    def keep_margin(slot, c, value):
        margin3[slot, c] = value

    def fold(z):
        return sum(pltpu.roll(z[b * nv : (b + 1) * nv], (z.shape[1] - b * nv) % z.shape[1], 1) if b else z[:nv] for b in range(H))

    def flat(ref, first, count):
        return ref[first : first + count].reshape(count * comps * cy, lanes)

    chunks = range(0, AFTER + 1, 2)
    octet_margins = [x2[slot, c, top, :] for slot in range(AFTER + 1) for c in range(comps)]
    margin_h2, margin_l2 = split(jnp.concatenate(octet_margins, axis=0))

    def product(other):
        margin, rows = other
        main = dot(margin_h2, jnp.concatenate(margin, axis=1), TN)
        for first in chunks:
            both = jnp.concatenate([flat(ref, first, 2) for ref in rows], axis=1)
            main = main + dot(turned[first // 2], both, NN)
        main = fold(main)
        return main[:, :nv], main[:, lanes : lanes + nv]

    def gram_m():
        for first in chunks:
            turned[first // 2] = flat(high2, first, 2).T
        main, mixed = product(((margin_h2, margin_l2), (high2, low2)))
        return main + (mixed + mixed.T)

    def gram_n():
        margin = split(margin3[...].reshape((AFTER + 1) * comps * 8, lanes))
        out = sum(product((margin, (high3, low3))))
        return 0.5 * (out + out.T)

    gram = gram_m()
    pad = jnp.zeros((nv, lanes - nv), F32)
    inverse = inverse_factor(jnp.concatenate([gram, pad], axis=1), nv, 8)[:, :nv]
    apply(twice, range(HEAD), range(HEAD), image_rows, keep_margin)
    inverse = jnp.where(iota((nv, nv), 0) < rank_ref[0, 0], inverse, 0.0)
    image = gram_n()

    def rim(strip, first, block):
        def rows_of(slot, weighted):
            out = []
            for at, weight_at in ((mid, slice(0, cy)), (top, slice(cy, cy + 8))):
                for c in range(comps):
                    rows = x2[slot, c, at, :]
                    if weighted:
                        rows = rows * (coef[slot, c, weight_at, :] + coef[slot, comps, weight_at, :])
                    out.append(rows)
            return out

        pad = [jnp.zeros((8, lanes), F32)]
        turned = [half.T for half in split(jnp.concatenate(rows_of(strip, True) + pad, axis=0))]
        total = jnp.zeros((2 * nv, 2 * lanes), F32)
        for i in range(H):
            margin = split(jnp.concatenate([x2[first + i, c, top, :] for c in range(comps)] + pad, axis=0))
            own = [
                jnp.concatenate([ref[first + i, c] for c in range(comps)] + [rest], axis=0)
                for ref, rest in zip((high2, low2), margin)
            ]
            other = jnp.concatenate([half[i * nv : (i + 1) * nv] for half in turned], axis=0)
            total = total + dot(other, jnp.concatenate(own, axis=1), NN)
        total = total[:nv] + total[nv:]
        total = total[:, :lanes] + total[:, lanes:]
        return total[:, block * nv : (block + 1) * nv].T

    rim_next = rim(TAIL, OWN - H, H - 1) * has_after
    rim_prev = rim(HEAD, 0, 0) * has_before

    start = start_ref[...]
    k2 = start.shape[0]
    products = dot3(jnp.concatenate([inverse.T, start], axis=0), inverse, NN)
    pack_ref[0, :nv] = jnp.concatenate([rim_prev, 0.5 * image, rim_next, products[:nv]], axis=1)
    starts = [products[nv + i : nv + i + 8] for i in range(0, k2, 8)]
    pad = jnp.zeros((8, lanes - nv * len(starts)), F32)
    pack_ref[0, nv:] = jnp.concatenate(starts + [pad], axis=1)


def prolong(coefs, high_ref, low_ref, out_ref, buf, sems):
    k2, nv = coefs.shape
    comps, cx = buf.shape[0], buf.shape[2]
    cy = buf.shape[3]
    own = cx // H
    tiled = jnp.concatenate([coefs] * H, axis=1)
    tiled = jnp.broadcast_to(tiled[:, None, :], (k2, 8, H * nv)).reshape(8 * k2, H * nv)
    same = lax.rem(iota(tiled.shape, 0), 8) == iota(tiled.shape, 1) // nv
    high, low = split(jnp.where(same, tiled, 0.0))
    left = jnp.concatenate([high, low, high], axis=1)
    copies = []
    for c in range(comps):
        for p in range(0, own, 2):
            bh = jnp.concatenate([high_ref[p, c], high_ref[p + 1, c]], axis=0)
            bl = jnp.concatenate([low_ref[p, c], low_ref[p + 1, c]], axis=0)
            both = dot(left, jnp.concatenate([bh, bh, bl], axis=1), NT)
            for i in range(2):
                out = both[:, i * cy : (i + 1) * cy].reshape(k2, 8, cy)
                buf[c, :, pl.ds(p + i, H, stride=own), :] = out[:, :H]
        copies.append(pltpu.make_async_copy(buf.at[c], out_ref.at[:, c], sems.at[c]))
        copies[-1].start()
    for copy in copies:
        copy.wait()


def level_kernel(spans, order, factor, *refs):
    parts, (high_ref, low_ref, out_ref, packs, buf, sems) = refs[:-6], refs[-6:]
    k2 = buf.shape[1]
    nv = packs.shape[1] - 8
    n = spans * nv
    s = lax.axis_index("sub")
    index = 0
    for part in parts:
        for i in range(part.shape[0]):
            packs[order[index]] = part[i]
            index += 1
    lane = iota((nv, 128), 1)

    def placed(block, offset, first, last):
        rolled = pltpu.roll(block, offset % 128, 1) if offset % 128 else block
        at = iota(block.shape, 1) - offset
        tiles = [jnp.where((at + m >= first) & (at + m < last), rolled, 0.0) for m in range(0, n, 128)]
        return jnp.concatenate(tiles, axis=1)

    rows, products = [], []
    u = jnp.zeros((k2, n), F32)
    for b in range(spans):
        pack = packs[jnp.bitwise_xor(s, b)]
        rows.append(placed(pack[:nv], nv * (b - 1), 0, 3 * nv))
        products.append(placed(pack[:nv], nv * (b - 3), 3 * nv, 4 * nv))
        starts = [placed(pack[nv:], nv * (b - i), nv * i, nv * i + nv) for i in range(k2 // 8)]
        u = u + jnp.concatenate(starts, axis=0)
    rows = jnp.concatenate(rows, axis=0)
    full = split(rows + rows.T)
    products = split(jnp.concatenate(products, axis=0))

    def times(x, halves):
        xh, xl = split(x)
        out = dot(jnp.concatenate([xh, xl], axis=0), halves[0], NN)
        return out[:k2] + (out[k2:] + dot(xh, halves[1], NN))

    z = times(times(times(u, full), products), full)
    w = times(z, products)
    gram = dot3(w, z, NT)
    gram = jnp.concatenate([gram, jnp.zeros((k2, 128 - k2), F32)], axis=1)
    own = pltpu.roll(w, lax.rem(n - nv * s, n), 1)[:, :nv]
    coefs = dot3(inverse_factor(gram, k2, k2)[:, :k2], factor * own, NN)
    prolong(coefs, high_ref, low_ref, out_ref, buf, sems)


def pairs(count, offset):
    return [q for i in range(offset, count - 1, 2) for q in ((i, i + 1), (i + 1, i))]


def from_behind(block, axis, distance):
    devices = range(lax.axis_size(axis))
    return lax.ppermute(block, axis, [(i - distance, i) for i in devices if i - distance in devices])


def level_coefs(pack, nv, k2, factor):
    highest = lax.Precision.HIGHEST
    rim_prev, half, rim_next, product = (pack[:nv, nv * i : nv * i + nv] for i in range(4))
    u = jnp.concatenate([pack[nv:, nv * i : nv * i + nv] for i in range(k2 // 8)], axis=0).T
    own = half + half.T
    rim = rim_next + from_behind(rim_prev, "sub", -1).T
    rim_before = from_behind(rim, "sub", 1)
    for step in range(2):
        z = jnp.dot(own, u, precision=highest)
        z = z + jnp.dot(rim, from_behind(u, "sub", -1), precision=highest)
        z = z + jnp.dot(rim_before.T, from_behind(u, "sub", 1), precision=highest)
        u = jnp.dot(product, z, precision=highest)
    lower = jnp.linalg.cholesky(lax.psum(jnp.dot(z.T, u, precision=highest), "sub"))
    return factor * lax.linalg.triangular_solve(lower, u.T, left_side=True, lower=True)


def in_vmem(x):
    return pltpu.with_memory_space_constraint(x, pltpu.VMEM)


def call(kernel, out_shape, scratch, name, in_specs=None, **more):
    return pl.pallas_call(
        kernel,
        out_shape=out_shape,
        scratch_shapes=scratch,
        compiler_params=pltpu.CompilerParams(vmem_limit_bytes=VMEM_MIB * MIB),
        name=name,
        **({"in_specs": in_specs} if in_specs else {}),
        **more,
    )


def on_device(start_vectors, stiffness, coupling, kept_ranks, level_start):
    spans, sects = lax.axis_size("sub"), lax.axis_size("sec")
    nv, comps, cx, cy = start_vectors.shape
    k2 = level_start.shape[1]
    channels = comps + 1
    slots = slots_of(cx)[-1] + 1
    shape = jax.ShapeDtypeStruct
    vmem = pl.BlockSpec(memory_space=pltpu.VMEM)
    hbm = pl.BlockSpec(memory_space=pltpu.HBM)

    pieces = (cx // H + 2) * comps + 1
    inputs = (start_vectors, stiffness, coupling, level_start.T)
    sec_shape = shape((-(-pieces // 2) * 8, cy), BF16)
    own, kt, sec_a, sec_b, start, narrow = call(
        pack_kernel,
        (shape((cx // H + 2, comps, cy, H * nv), BF16), shape((cy, channels * cx), BF16), sec_shape, sec_shape)
        + (shape((k2, nv), F32), shape((2 * H * channels * cy // (H * nv), cy), BF16)),
        [
            pltpu.VMEM((comps, nv, cx, cy), BF16),
            pltpu.VMEM(stiffness.shape, BF16),
            pltpu.VMEM(coupling.shape, BF16),
            pltpu.VMEM((comps, nv * (cx + 8), cy), F32),
            pltpu.VMEM((channels * cx, cy), F32),
            pltpu.SemaphoreType.DMA((comps + 3,)),
        ],
        "pack",
        [hbm] * 4,
    )(*(pltpu.with_memory_space_constraint(x, pltpu.HBM) for x in inputs))
    sec_a = lax.ppermute(sec_a, "sec", pairs(sects, 0))
    sec_b = lax.ppermute(sec_b, "sec", pairs(sects, 1))

    def edge(*refs):
        edge_kernel(cx, *refs)

    sub_shape = shape((comps * cy + narrow.shape[0] + channels * 8, H * nv), BF16)
    sub_a, sub_b = call(edge, (sub_shape, sub_shape), [], "edge")(own, narrow, sec_a, sec_b)
    sub_a = lax.ppermute(sub_a, "sub", pairs(spans, 0))
    sub_b = lax.ppermute(sub_b, "sub", pairs(spans, 1))

    def fine(*refs):
        fine_kernel((spans, sects), *refs)

    rows = shape((slots, comps, cy + 16, H * nv), F32)
    weights = shape((slots, channels, cy + 8, H * nv), F32)
    half = shape((slots - 2, comps, cy, H * nv), BF16)
    v0, coef, x1 = (in_vmem(x) for x in call(prep_kernel, (rows, weights, rows), [], "prep")(own, kt))
    pack, high, low, *_ = call(
        fine,
        (shape((1, nv + 8, cy), F32), half, half, rows, weights, rows),
        [
            pltpu.VMEM(rows.shape, F32),
            pltpu.VMEM(rows.shape, F32),
            pltpu.VMEM(((slots - 2) // 2, H * nv, 2 * comps * cy), BF16),
            pltpu.VMEM(half.shape, BF16),
            pltpu.VMEM(half.shape, BF16),
            pltpu.VMEM((slots - 2, comps, 8, H * nv), F32),
        ],
        "fine",
        [pl.BlockSpec(memory_space=pltpu.SMEM)] + [vmem] * 9,
        input_output_aliases={2: 3, 3: 4, 4: 5},
    )(kept_ranks, start, v0, coef, x1, kt, sec_a, sec_b, sub_a, sub_b)

    factor = math.sqrt(spans * comps * (cx + 2 * H) * (cy + 2 * H))
    result = shape((k2, comps, cx, cy), F32)
    tiles = [pltpu.VMEM((comps, k2, cx, cy), F32), pltpu.SemaphoreType.DMA((comps,))]
    if spans != 8:

        def prolong_kernel(coefs_ref, *refs):
            prolong(coefs_ref[...], *refs)

        coefs = level_coefs(pack[0], nv, k2, factor)
        return call(prolong_kernel, result, tiles, "prolong", [vmem] * 3, out_specs=hbm)(coefs, high, low)

    def swapped(block, bit):
        return lax.ppermute(block, "sub", [(i, i ^ bit) for i in range(spans)])

    far = swapped(pack, 4)
    both = jnp.concatenate([pack, far])
    parts = [both] + [swapped(both, bit) for bit in (2, 1, 3)]
    order = [high_bit ^ bit for bit in (0, 2, 1, 3) for high_bit in (0, 4)]

    def level(*refs):
        level_kernel(spans, order, factor, *refs)

    packs = pltpu.VMEM((spans,) + pack.shape[1:], F32)
    return call(level, result, [packs] + tiles, "level", [vmem] * 6, out_specs=hbm)(*parts, high, low)


def solution(mesh):
    placed = (
        P(None, None, "sub", "sec"),
        P(None, "sub", "sec"),
        P("sub", "sec"),
        P("sub", "sec"),
        P("sub", None),
    )
    return jax.shard_map(
        on_device,
        mesh=mesh,
        in_specs=placed,
        out_specs=P(None, None, "sub", "sec"),
        check_vma=False,
    )
```
